512 devices in a mesh: grid: 64 (over y, z), lev: 4 (over x), side: 2 (over core).
Axes of the slice: x: 4, y: 8, z: 8, core: 2. Of those that a mesh axis runs over, the one named last changes fastest.
Arguments:
- model_state: float32 [2, 8, 6, 524288], P('side', 'lev', None, 'grid'), may hold values from -6 to 6
- terrain_level: int32 [2, 8, 524288], P('side', None, 'grid'), may hold values from 0 to 7
- panel_owner: int32 [65536, 1], P('grid'), may hold values from 0 to 63, as said below
- panel_cell: int32 [65536], P('grid'), may hold values from 0 to 8191
- block_weight: float32 [4096, 16, 128], P('grid'), may hold values from 0 to 0.015625
- block_owner: int32 [4096, 1], P('grid'), may hold values from 0 to 63, as said below
- block_row: int32 [4096], P('grid'), may hold values from 0 to 511
Outputs:
- new_state: float32 [2, 8, 6, 524288], P('side', 'lev', None, 'grid')
The draws below stay inside these ranges and needn't reach their ends.
Inputs may be any that keep to these rules, and one draw needn't show every extreme that they name: `panel_owner`: the panel slots of nest tile t name only the global tiles (t - 1), (t + 1) and (t + 32), taken modulo 64; within the 1024 slots of one nest tile no global tile is named more than 512 times, and some global tile is named exactly that often. `block_owner`: the blocks of nest tile t name only the global tiles (t - 1), (t + 1) and (t + 32), taken modulo 64; within the 64 blocks of one nest tile no global tile is named more than 32 times, and some global tile is named exactly that often.
All inputs are finite; a program needn't handle non-finite values.
Results may differ from the reference program's by a relative error of at most 0.00005.
Values sent between devices are 32-bit elements; how exact they have to be, the bound alone decides.
A program may use at most 192 MiB of HBM per device.

```python
import jax
import jax.numpy as jnp
from jax import lax

FIELDS = 6
CELL_DEV = 8192
BLOCK_FINE = 128
BLOCK_COARSE = 16
LEVELS = 8
CELLS = 524288
BLOCKS = 4096
BLOCK_CAP = 32
SLOT_CAP = 512
PANEL_DEV = 1024
PANELS = 65536
ROW_BLOCKS = 512
N_GRID = 64


def owner_lists(key, capacity):
    count = 2 * capacity
    offsets = jnp.array([N_GRID - 1, 1, N_GRID // 2], jnp.int32)
    key_first, key_second, key_order = jax.random.split(key, 3)
    first_pick = jax.random.randint(key_first, (N_GRID,), 0, 3, dtype=jnp.int32)
    second_count = jax.random.randint(key_second, (N_GRID,), 0, capacity + 1, dtype=jnp.int32)
    position = jnp.arange(count, dtype=jnp.int32)[None, :]
    ranked = jnp.where(position < capacity, 0, jnp.where(position < capacity + second_count[:, None], 1, 2))
    picked = jnp.mod(first_pick[:, None] + ranked, 3).astype(jnp.int32)
    tile_keys = jax.random.split(key_order, N_GRID)
    orders = jax.vmap(lambda single: jax.random.permutation(single, count))(tile_keys)
    shuffled = jnp.take_along_axis(picked, orders.astype(jnp.int32), axis=1)
    tiles = jnp.arange(N_GRID, dtype=jnp.int32)[:, None]
    owners = jnp.mod(tiles + jnp.take(offsets, shuffled), N_GRID)
    return owners.reshape(-1, 1).astype(jnp.int32)


def draw_panel_owner(key, part):
    return owner_lists(jax.random.fold_in(key, 11), SLOT_CAP)


def draw_block_owner(key, part):
    return owner_lists(jax.random.fold_in(key, 23), BLOCK_CAP)


def with_ends(entries, stream_key, low, top_value):
    place = [jax.random.randint(jax.random.fold_in(stream_key, axis), (), 0, length) for axis, length in enumerate(entries.shape)]
    widest = entries.shape.index(max(entries.shape))
    beside = place[:widest] + [(place[widest] + 1) % entries.shape[widest]] + place[widest + 1:]
    return entries.at[tuple(place)].set(low).at[tuple(beside)].set(top_value)


def level_of(stream_key, shape, cuts, least, high):
    def one(dim, parts):
        steps = jax.random.uniform(jax.random.fold_in(jax.random.fold_in(stream_key, 6), dim), (parts,), jnp.float32, least / len(cuts), high / len(cuts))
        return jnp.repeat(jnp.exp(steps), shape[dim] // parts).reshape((-1,) + (1,) * (len(shape) - dim - 1))

    loudness = one(*cuts[0])
    for cut in cuts[1:]:
        loudness = loudness * one(*cut)
    return loudness


def gaussian(own_key, extent, width, reach, cuts=(), kind=jnp.bfloat16):
    values = width * jax.random.normal(own_key, extent, jnp.float32)
    if cuts:
        values = values * level_of(own_key, extent, cuts, -0.22, 0.18)
    return jnp.clip(values, -reach, reach).astype(kind)


def setup_inputs(seed: int = 0) -> dict:
    splits = jax.random.split(jax.random.key(seed), 8)
    model_state = gaussian(splits[0], (2, LEVELS, FIELDS, CELLS), 1.0, 6.0, ((0, 2), (1, 4), (3, 64)), jnp.float32)
    terrain_level = with_ends(jax.random.randint(splits[1], (2, LEVELS, CELLS), 0, LEVELS), jax.random.fold_in(splits[1], 1), 0, LEVELS - 1).astype(jnp.int32)
    panel_owner = draw_panel_owner(jax.random.fold_in(splits[7], 71), 0)
    panel_cell = with_ends(jax.random.randint(splits[3], (PANELS,), 0, CELL_DEV), jax.random.fold_in(splits[3], 1), 0, CELL_DEV - 1).astype(jnp.int32)
    block_weight = jnp.clip(0.015625 * jax.random.uniform(splits[4], (BLOCKS, BLOCK_COARSE, BLOCK_FINE), jnp.float32) ** level_of(splits[4], (BLOCKS, BLOCK_COARSE, BLOCK_FINE), ((0, 64),), -0.2, 0.2), 0.0, 0.015625)
    block_owner = draw_block_owner(jax.random.fold_in(splits[7], 71), 0)
    block_row = with_ends(jax.random.randint(splits[6], (BLOCKS,), 0, ROW_BLOCKS), jax.random.fold_in(splits[6], 1), 0, ROW_BLOCKS - 1).astype(jnp.int32)
    return dict(model_state=model_state, terrain_level=terrain_level, panel_owner=panel_owner, panel_cell=panel_cell, block_weight=block_weight, block_owner=block_owner, block_row=block_row)


def remap_levels(fields, terrain):
    indices = jnp.broadcast_to(terrain[:, None, :].astype(jnp.int32), fields.shape)
    return jnp.take_along_axis(fields, indices, axis=0)


def reference(model_state, terrain_level, panel_owner, panel_cell, block_weight, block_owner, block_row):
    coarse = model_state[0]
    nested = model_state[1]
    coarse_moved = remap_levels(coarse, terrain_level[0])
    nested_moved = remap_levels(nested, terrain_level[1])
    panel_index = (panel_owner[:, 0] * CELL_DEV + panel_cell).astype(jnp.int32)
    panel_values = coarse_moved[:, :, panel_index]
    blocks = nested_moved.reshape(LEVELS, FIELDS, BLOCKS, BLOCK_FINE)
    partial_sums = jnp.einsum("brj,kfbj->kfbr", block_weight, blocks, precision=lax.Precision.HIGHEST)
    block_mass = jnp.sum(block_weight, axis=2)
    target = (block_owner[:, 0] * CELL_DEV + block_row * BLOCK_COARSE)[:, None] + jnp.arange(BLOCK_COARSE, dtype=jnp.int32)[None, :]
    target = target.reshape(-1).astype(jnp.int32)
    feedback = jnp.zeros_like(coarse).at[:, :, target].add(partial_sums.reshape(LEVELS, FIELDS, BLOCKS * BLOCK_COARSE))
    weight_sum = jnp.zeros((CELLS,), jnp.float32).at[target].add(block_mass.reshape(-1))
    new_coarse = (coarse + feedback) / (1.0 + weight_sum)
    nest_tiles = nested.reshape(LEVELS, FIELDS, N_GRID, CELL_DEV)
    rim_values = panel_values.reshape(LEVELS, FIELDS, N_GRID, PANEL_DEV)
    blended = 0.5 * (nest_tiles[..., :PANEL_DEV] + rim_values)
    new_nested = jnp.concatenate([blended, nest_tiles[..., PANEL_DEV:]], axis=3).reshape(LEVELS, FIELDS, CELLS)
    return jnp.stack([new_coarse, new_nested])
```

```python
import functools

import jax
import jax.numpy as jnp
from jax import lax
from jax.experimental import pallas as pl
from jax.experimental.pallas import tpu as pltpu
from jax.sharding import PartitionSpec as P

MESH = pl.DeviceIdType.MESH
LANES = 128
FIELD_ROWS = 8
MASS_ROW = 6
FLIPPED = (1, 0, 2)


def place(grid, lev, side):
    return {"grid": grid, "lev": lev, "side": side}


def exchange_kernel(
    sizes,
    cell_ref,
    owner_ref,
    block_ref,
    state_ref,
    terrain_ref,
    weight_ref,
    landed_ref,
    landed_block_ref,
    rim_ref,
    rows,
    part,
    served,
    asked,
    sums,
    sums_in,
    merged,
    merged_in,
    ask_send,
    ask_recv,
    block_send,
    block_recv,
    value_send,
    value_recv,
    sum_send,
    sum_recv,
    merged_send,
    merged_recv,
):
    tiles, groups, fields, cell_rows, slot_rows = sizes
    tile = lax.axis_index("grid")
    group = lax.axis_index("lev")
    side = lax.axis_index("side")
    partners = [
        lax.rem(tile + step, tiles) for step in (tiles - 1, 1, tiles // 2)
    ]
    peers = [lax.rem(group + step, groups) for step in range(1, groups)]
    stride = 2 * cell_rows

    barrier = pltpu.get_barrier_semaphore()
    for partner in partners:
        pl.semaphore_signal(
            barrier, inc=1, device_id=place(partner, group, 1 - side), device_id_type=MESH
        )

    @pl.when(side == 0)
    def _():
        for partner in partners:
            pl.semaphore_signal(
                barrier, inc=1, device_id=place(partner, group, side), device_id_type=MESH
            )

    @pl.when(side == 1)
    def _():
        for peer in peers:
            pl.semaphore_signal(
                barrier, inc=1, device_id=place(tile, peer, side), device_id_type=MESH
            )

    def value_copy(source, number):
        return pltpu.make_async_remote_copy(
            src_ref=source,
            dst_ref=landed_ref.at[FLIPPED[number]],
            send_sem=value_send.at[number],
            recv_sem=value_recv.at[FLIPPED[number]],
            device_id=place(partners[number], group, 1 - side),
            device_id_type=MESH,
        )

    def value_arrival(number):
        return pltpu.make_async_remote_copy(
            src_ref=served.at[number],
            dst_ref=landed_ref.at[number],
            send_sem=value_send.at[number],
            recv_sem=value_recv.at[number],
            device_id=place(partners[number], group, 1 - side),
            device_id_type=MESH,
        )

    row_number = lax.broadcasted_iota(jnp.int32, (FIELD_ROWS, LANES), 0)

    @pl.when(side == 0)
    def _():
        pl.semaphore_wait(barrier, len(partners) * 2)
        asks = []
        for number, partner in enumerate(partners):
            for source, target, sent, received in (
                (cell_ref, asked, ask_send, ask_recv),
                (block_ref, landed_block_ref, block_send, block_recv),
            ):
                copy = pltpu.make_async_remote_copy(
                    src_ref=source,
                    dst_ref=target.at[FLIPPED[number]],
                    send_sem=sent.at[number],
                    recv_sem=received.at[FLIPPED[number]],
                    device_id=place(partner, group, side),
                    device_id_type=MESH,
                )
                copy.start()
                asks.append(copy)
        rows[...] = jnp.zeros_like(rows)

        def fill(number, carry):
            lanes = pl.ds(pl.multiple_of(number * LANES, LANES), LANES)
            supply = terrain_ref[:, lanes].astype(jnp.float32)
            for level in range(2):
                rows[level * cell_rows + number, 0:fields, :] = state_ref[
                    pl.ds(number * 2 + level, fields, stride=stride), :
                ]
                turned = pltpu.roll(
                    supply, lax.rem(fields + FIELD_ROWS - 2 * group - level, FIELD_ROWS), axis=0
                )
                rows[level * cell_rows + number, fields : fields + 1, :] = turned[
                    fields : fields + 1, :
                ]
            return carry

        lax.fori_loop(0, cell_rows, fill, 0)
        for number, partner in enumerate(partners):
            pltpu.make_async_remote_copy(
                src_ref=cell_ref,
                dst_ref=asked.at[number],
                send_sem=ask_send.at[number],
                recv_sem=ask_recv.at[number],
                device_id=place(partner, group, side),
                device_id_type=MESH,
            ).wait_recv()
            lane_of = []
            row_of = []
            for slot_row in range(slot_rows):
                wanted = jnp.broadcast_to(
                    asked[number, slot_row : slot_row + 1, :], (FIELD_ROWS, LANES)
                )
                lane_of.append(wanted & (LANES - 1))
                row_of.append(wanted >> 7)

            def scan(step, found):
                out = []
                values = [rows[level * cell_rows + step] for level in range(2)]
                for slot_row in range(slot_rows):
                    here = row_of[slot_row] == step
                    for level in range(2):
                        picked = jnp.take_along_axis(
                            values[level], lane_of[slot_row], axis=1, mode="promise_in_bounds"
                        )
                        out.append(jnp.where(here, picked, found[slot_row * 2 + level]))
                return tuple(out)

            found = lax.fori_loop(
                0,
                cell_rows,
                scan,
                tuple(jnp.zeros((FIELD_ROWS, LANES), jnp.float32) for _ in range(2 * slot_rows)),
            )
            for slot_row in range(slot_rows):
                for level in range(2):
                    served[number, level, :, slot_row * LANES : (slot_row + 1) * LANES] = found[
                        slot_row * 2 + level
                    ]
            value_copy(served.at[number], number).start()
        for copy in asks:
            copy.wait_send()
        for number, partner in enumerate(partners):
            pltpu.make_async_remote_copy(
                src_ref=block_ref,
                dst_ref=landed_block_ref.at[number],
                send_sem=block_send.at[number],
                recv_sem=block_recv.at[number],
                device_id=place(partner, group, side),
                device_id_type=MESH,
            ).wait_recv()
        for number in range(len(partners)):
            value_copy(served.at[number], number).wait_send()
            value_arrival(number).wait_recv()

    @pl.when(side == 1)
    def _():
        rows[...] = jnp.zeros_like(rows)

        def fill(number, carry):
            for level in range(2):
                rows[level * cell_rows + number, 0:fields, :] = state_ref[
                    pl.ds(number * 2 + level, fields, stride=stride), :
                ]
            return carry

        lax.fori_loop(0, cell_rows, fill, 0)
        levels = 2 * groups
        mass = [
            jnp.where((row_number == MASS_ROW) & (level == 2 * group), 1.0, 0.0)
            for level in range(levels)
        ]
        lane_group = (
            lax.broadcasted_iota(jnp.int32, (levels * FIELD_ROWS, LANES), 1) >> 4
        )

        def block_group(number, carry):
            stack = []
            for member in range(8):
                block = number * 8 + member
                lanes = pl.ds(pl.multiple_of(block * LANES, LANES), LANES)
                low = rows[block]
                high = rows[cell_rows + block]
                supply = terrain_ref[:, lanes]
                for level in range(levels):
                    source = jnp.broadcast_to(supply[level : level + 1, :], (FIELD_ROWS, LANES))
                    stack.append(
                        jnp.where(
                            source == 2 * group,
                            low,
                            jnp.where(source == 2 * group + 1, high, 0.0),
                        )
                        + mass[level]
                    )
            values = jnp.concatenate(stack, axis=0)
            coarse_part = values.astype(jnp.bfloat16)
            fine_part = (values - coarse_part.astype(jnp.float32)).astype(jnp.bfloat16)
            left = jnp.concatenate([coarse_part, fine_part], axis=1)
            weight = weight_ref[pl.ds(number * 8, 8)].reshape(8 * 16, LANES)
            weight_high = weight.astype(jnp.bfloat16)
            weight_low = (weight - weight_high.astype(jnp.float32)).astype(jnp.bfloat16)
            right = jnp.concatenate(
                [
                    jnp.concatenate([weight_high, weight_high], axis=1),
                    jnp.concatenate([weight_low, weight_low], axis=1),
                ],
                axis=0,
            )
            product = lax.dot_general(
                left, right, (((1,), (1,)), ((), ())), preferred_element_type=jnp.float32
            )
            total = jnp.zeros((levels * FIELD_ROWS, LANES), jnp.float32)
            for member in range(8):
                span = product[member * levels * FIELD_ROWS : (member + 1) * levels * FIELD_ROWS]
                total = jnp.where(
                    lane_group == member, span[:, :LANES] + span[:, LANES:], total
                )
            lanes = pl.ds(pl.multiple_of(number * LANES, LANES), LANES)
            for level in range(levels):
                part[level // 2, level % 2, :, lanes] = total[
                    level * FIELD_ROWS : (level + 1) * FIELD_ROWS
                ]
            return carry

        lax.fori_loop(0, cell_rows // 8, block_group, 0)
        pl.semaphore_wait(barrier, len(partners) + len(peers))

        def sum_copy(number):
            return pltpu.make_async_remote_copy(
                src_ref=part.at[peers[number]],
                dst_ref=sums_in.at[number],
                send_sem=sum_send.at[number],
                recv_sem=sum_recv.at[number],
                device_id=place(tile, peers[number], side),
                device_id_type=MESH,
            )

        def merged_copy(number):
            return pltpu.make_async_remote_copy(
                src_ref=merged,
                dst_ref=merged_in.at[number],
                send_sem=merged_send.at[number],
                recv_sem=merged_recv.at[number],
                device_id=place(tile, peers[number], side),
                device_id_type=MESH,
            )

        for number in range(len(peers)):
            sum_copy(number).start()
        for number in range(len(peers)):
            sum_copy(number).wait_recv()
        own = part[group]
        for number in range(len(peers)):
            own = own + sums_in[number]
        sums[...] = own
        for number in range(len(partners)):
            value_copy(sums, number).start()
        for number in range(len(partners)):
            value_arrival(number).wait_recv()
        for slot_row in range(slot_rows):
            lanes = slice(slot_row * LANES, (slot_row + 1) * LANES)
            owner = jnp.broadcast_to(owner_ref[slot_row : slot_row + 1, :], (FIELD_ROWS, LANES))
            for level in range(2):
                merged[level, :, lanes] = jnp.where(
                    owner == partners[0],
                    landed_ref[0, level, :, lanes],
                    jnp.where(
                        owner == partners[1],
                        landed_ref[1, level, :, lanes],
                        landed_ref[2, level, :, lanes],
                    ),
                )
        for number in range(len(peers)):
            merged_copy(number).start()
        for number in range(len(peers)):
            merged_copy(number).wait_recv()
        for slot_row in range(slot_rows):
            lanes = slice(slot_row * LANES, (slot_row + 1) * LANES)
            for level in range(2):
                wanted = jnp.broadcast_to(
                    merged[level, fields : fields + 1, lanes], (FIELD_ROWS, LANES)
                )
                value = jnp.zeros((FIELD_ROWS, LANES), jnp.float32)
                for there in range(2):
                    value = jnp.where(
                        wanted == (2 * group + there).astype(jnp.float32),
                        merged[there, :, lanes],
                        value,
                    )
                    for number in range(len(peers)):
                        origin = lax.rem(group + groups - 1 - number, groups)
                        value = jnp.where(
                            wanted == (2 * origin + there).astype(jnp.float32),
                            merged_in[number, there, :, lanes],
                            value,
                        )
                rim_ref[level, :, lanes] = value
        for number in range(len(peers)):
            sum_copy(number).wait_send()
            merged_copy(number).wait_send()
        for number in range(len(partners)):
            value_copy(sums, number).wait_send()


def finish_kernel(
    sizes, place_ref, block_ref, state_ref, landed_ref, rim_ref, out_ref, total
):
    fields, cell_rows, slot_rows, blocks = sizes
    tile = place_ref[0]
    side = place_ref[1]
    stride = 2 * cell_rows

    @pl.when(side == 0)
    def _():
        total[...] = jnp.zeros_like(total)
        lane_group = lax.broadcasted_iota(jnp.int32, (FIELD_ROWS, LANES), 1) >> 4
        for number in range(3):

            def add(block, carry):
                @pl.when(block_ref[number, 0, block] == tile)
                def _():
                    run = block_ref[number, 0, blocks + block]
                    target = run & 7
                    shift = ((target - block) & 7) * 16
                    lanes = pl.ds(pl.multiple_of((block >> 3) * LANES, LANES), LANES)
                    for level in range(2):
                        value = pltpu.roll(landed_ref[number, level, :, lanes], shift, axis=1)
                        row = level * cell_rows + (run >> 3)
                        total[row] = total[row] + jnp.where(lane_group == target, value, 0.0)

                return carry

            lax.fori_loop(0, blocks, add, 0)

        def close(number, carry):
            mass = total[number, MASS_ROW : MASS_ROW + 1, :]
            weight = jnp.broadcast_to(1.0 + mass, (fields, LANES))
            for level in range(2):
                where = pl.ds(number * 2 + level, fields, stride=stride)
                out_ref[where, :] = (
                    state_ref[where, :] + total[level * cell_rows + number, 0:fields, :]
                ) / weight
            return carry

        lax.fori_loop(0, cell_rows, close, 0)

    @pl.when(side == 1)
    def _():
        out_ref[...] = state_ref[...]
        for number in range(slot_rows):
            for level in range(2):
                where = pl.ds(number * 2 + level, fields, stride=stride)
                out_ref[where, :] = 0.5 * (
                    state_ref[where, :]
                    + rim_ref[level, 0:fields, number * LANES : (number + 1) * LANES]
                )


def on_device(
    tiles, groups,
    model_state, terrain_level, panel_owner, panel_cell, block_weight, block_owner, block_row
):
    _, lev_dev, fields, cells = model_state.shape
    cell_rows = cells // LANES
    slot_rows = panel_cell.shape[0] // LANES
    slots = panel_cell.shape[0]
    blocks = block_row.shape[0]
    state = (
        model_state[0]
        .transpose(1, 0, 2)
        .reshape(fields, lev_dev, cell_rows, LANES)
        .transpose(0, 2, 1, 3)
        .reshape(fields * cell_rows * lev_dev, LANES)
    )
    cell_wanted = panel_cell.reshape(slot_rows, LANES)
    cell_owner = panel_owner.reshape(slot_rows, LANES)
    block_place = jnp.concatenate([block_owner.reshape(-1), block_row]).reshape(1, -1)
    vmem = pl.BlockSpec(memory_space=pltpu.VMEM)
    smem = pl.BlockSpec(memory_space=pltpu.SMEM)
    tile_shape = (2, FIELD_ROWS, slots)
    dma = pltpu.SemaphoreType.DMA
    landed, landed_block, rim = pl.pallas_call(
        functools.partial(
            exchange_kernel, (tiles, groups, fields, cell_rows, slot_rows)
        ),
        out_shape=(
            jax.ShapeDtypeStruct((3, *tile_shape), jnp.float32),
            jax.ShapeDtypeStruct((3, *block_place.shape), jnp.int32),
            jax.ShapeDtypeStruct(tile_shape, jnp.float32),
        ),
        in_specs=[vmem] * 6,
        out_specs=(vmem, vmem, vmem),
        scratch_shapes=[
            pltpu.VMEM((2 * cell_rows, FIELD_ROWS, LANES), jnp.float32),
            pltpu.VMEM((groups, *tile_shape), jnp.float32),
            pltpu.VMEM((3, *tile_shape), jnp.float32),
            pltpu.VMEM((3, slot_rows, LANES), jnp.int32),
            pltpu.VMEM(tile_shape, jnp.float32),
            pltpu.VMEM((groups - 1, *tile_shape), jnp.float32),
            pltpu.VMEM(tile_shape, jnp.float32),
            pltpu.VMEM((groups - 1, *tile_shape), jnp.float32),
            *[dma((3,))] * 6,
            *[dma((groups - 1,))] * 4,
        ],
        compiler_params=pltpu.CompilerParams(collective_id=0, has_side_effects=True),
    )(cell_wanted, cell_owner, block_place, state, terrain_level[0], block_weight)
    here = jnp.stack([lax.axis_index("grid"), lax.axis_index("side")]).astype(jnp.int32)
    out = pl.pallas_call(
        functools.partial(finish_kernel, (fields, cell_rows, slot_rows, blocks)),
        out_shape=jax.ShapeDtypeStruct(state.shape, jnp.float32),
        in_specs=[smem, smem, vmem, vmem, vmem],
        out_specs=vmem,
        scratch_shapes=[pltpu.VMEM((2 * cell_rows, FIELD_ROWS, LANES), jnp.float32)],
    )(here, landed_block, state, landed, rim)
    out = (
        out.reshape(fields, cell_rows, lev_dev, LANES)
        .transpose(0, 2, 1, 3)
        .reshape(fields, lev_dev, cells)
        .transpose(1, 0, 2)
    )
    return out[None]


def solution(mesh):
    in_specs = (
        P("side", "lev", None, "grid"),
        P("side", None, "grid"),
        P("grid", None),
        P("grid"),
        P("grid", None, None),
        P("grid", None),
        P("grid"),
    )
    out_specs = P("side", "lev", None, "grid")
    return jax.shard_map(
        functools.partial(on_device, mesh.shape["grid"], mesh.shape["lev"]),
        mesh=mesh,
        in_specs=in_specs,
        out_specs=out_specs,
        check_vma=False,
    )
```

```python
import functools

import jax
import jax.numpy as jnp
from jax import lax
from jax.experimental import pallas as pl
from jax.experimental.pallas import tpu as pltpu
from jax.sharding import PartitionSpec as P

MESH = pl.DeviceIdType.MESH
LANES = 128
FIELD_ROWS = 8
MASS_ROW = 6
FLIPPED = (1, 0, 2)


def place(grid, lev, side):
    return {"grid": grid, "lev": lev, "side": side}


def exchange_kernel(
    sizes,
    cell_hbm,
    owner_hbm,
    block_owner_hbm,
    block_row_hbm,
    state_hbm,
    terrain_hbm,
    weight_hbm,
    landed_hbm,
    landed_owner_hbm,
    landed_row_hbm,
    rim_ref,
    owner_ref,
    state_ref,
    terrain_ref,
    weight_ref,
    rows,
    table,
    supply_rows,
    part,
    served,
    asked,
    arrived,
    sums,
    sums_in,
    merged,
    merged_in,
    load_sem,
    ask_send,
    ask_recv,
    owner_send,
    owner_recv,
    row_send,
    row_recv,
    value_send,
    value_recv,
    sum_send,
    sum_recv,
    merged_send,
    merged_recv,
):
    tiles, groups, fields, cell_rows, slot_rows = sizes
    tile = lax.axis_index("grid")
    group = lax.axis_index("lev")
    side = lax.axis_index("side")
    partners = [
        lax.rem(tile + step, tiles) for step in (tiles - 1, 1, tiles // 2)
    ]
    peers = [lax.rem(group + step, groups) for step in range(1, groups)]
    stride = 2 * cell_rows
    span = fields * stride

    barrier = pltpu.get_barrier_semaphore()
    for partner in partners:
        pl.semaphore_signal(
            barrier, inc=1, device_id=place(partner, group, 1 - side), device_id_type=MESH
        )

    @pl.when(side == 0)
    def _():
        for partner in partners:
            pl.semaphore_signal(
                barrier, inc=1, device_id=place(partner, group, side), device_id_type=MESH
            )

    @pl.when(side == 1)
    def _():
        for peer in peers:
            pl.semaphore_signal(
                barrier, inc=1, device_id=place(tile, peer, side), device_id_type=MESH
            )

    load_state = pltpu.make_async_copy(state_hbm, state_ref, load_sem.at[0])
    load_terrain = pltpu.make_async_copy(terrain_hbm, terrain_ref, load_sem.at[1])
    load_weight = pltpu.make_async_copy(weight_hbm, weight_ref, load_sem.at[2])
    load_owner = pltpu.make_async_copy(owner_hbm, owner_ref, load_sem.at[3])
    load_state.start()
    load_terrain.start()

    def remote(source, target, sent, received, where):
        return pltpu.make_async_remote_copy(
            src_ref=source,
            dst_ref=target,
            send_sem=sent,
            recv_sem=received,
            device_id=where,
            device_id_type=MESH,
        )

    row_number = lax.broadcasted_iota(jnp.int32, (FIELD_ROWS, LANES), 0)

    @pl.when(side == 0)
    def _():
        def ask(number, slot):
            return remote(
                cell_hbm, asked.at[slot], ask_send.at[number], ask_recv.at[slot],
                place(partners[number], group, side),
            )

        def tell_owner(number, slot):
            return remote(
                block_owner_hbm, landed_owner_hbm.at[slot], owner_send.at[number],
                owner_recv.at[slot], place(partners[number], group, side),
            )

        def tell_row(number, slot):
            return remote(
                block_row_hbm, landed_row_hbm.at[slot], row_send.at[number],
                row_recv.at[slot], place(partners[number], group, side),
            )

        def serve(number, slot):
            return remote(
                served.at[number], arrived.at[slot], value_send.at[number],
                value_recv.at[slot], place(partners[number], group, 1 - side),
            )

        def feed(number):
            return remote(
                sums, landed_hbm.at[number], value_send.at[number],
                value_recv.at[number], place(partners[number], group, 1 - side),
            )

        pl.semaphore_wait(barrier, len(partners) * 2)
        for number in range(3):
            ask(number, FLIPPED[number]).start()
        for number in range(3):
            tell_owner(number, FLIPPED[number]).start()
            tell_row(number, FLIPPED[number]).start()
        load_terrain.wait()

        def fill(number, carry):
            mixed = jnp.zeros((FIELD_ROWS, LANES), jnp.float32)
            for member in range(4):
                lanes = pl.ds(pl.multiple_of((number * 4 + member) * LANES, LANES), LANES)
                turned = pltpu.roll(
                    terrain_ref[:, lanes].astype(jnp.float32),
                    lax.rem(2 * member + FIELD_ROWS - 2 * group, FIELD_ROWS),
                    axis=0,
                )
                mixed = jnp.where(row_number >> 1 == member, turned, mixed)
            supply_rows[pl.ds(pl.multiple_of(number * FIELD_ROWS, FIELD_ROWS), FIELD_ROWS), :] = (
                mixed
            )
            return carry

        lax.fori_loop(0, cell_rows // 4, fill, 0)
        load_state.wait()

        def split(number, carry):
            where = pl.ds(pl.multiple_of(number * stride, stride), stride)
            value = state_ref[where, :]
            high = value.astype(jnp.bfloat16)
            table[where, :LANES] = high
            table[where, LANES:] = (value - high.astype(jnp.float32)).astype(jnp.bfloat16)
            return carry

        lax.fori_loop(0, fields, split, 0)
        table[span:, :LANES] = supply_rows[...].astype(jnp.bfloat16)
        table[span:, LANES:] = jnp.zeros((stride, LANES), jnp.bfloat16)

        lane_number = lax.broadcasted_iota(jnp.int32, (LANES, LANES), 0)
        row_pair = lax.broadcasted_iota(jnp.int32, (stride, LANES), 0) >> 1
        for number in range(3):
            ask(number, number).wait_recv()

            def look(step, carry):
                ones = []
                masks = []
                for half in range(2):
                    wanted = asked[number, 2 * step + half]
                    ones.append(
                        jnp.where(
                            lane_number
                            == jnp.broadcast_to(wanted & (LANES - 1), (LANES, LANES)),
                            1.0,
                            0.0,
                        ).astype(jnp.bfloat16)
                    )
                    masks.append(row_pair == jnp.broadcast_to(wanted >> 7, (stride, LANES)))
                one_hot = jnp.concatenate(ones, axis=1)
                one_hot = jnp.concatenate([one_hot, one_hot], axis=0)
                found = jnp.dot(table[...], one_hot, preferred_element_type=jnp.float32)
                for half in range(2):
                    tile_even = jnp.zeros((FIELD_ROWS, LANES), jnp.float32)
                    tile_odd = tile_even
                    for field in range(fields + 1):
                        picked = jnp.where(
                            masks[half],
                            found[
                                field * stride : (field + 1) * stride,
                                half * LANES : (half + 1) * LANES,
                            ],
                            0.0,
                        )
                        total = jnp.sum(
                            picked.reshape(stride // FIELD_ROWS, FIELD_ROWS, LANES), axis=0
                        )
                        total = total + pltpu.roll(total, 4, axis=0)
                        total = total + pltpu.roll(total, 2, axis=0)
                        other = pltpu.roll(total, 1, axis=0)
                        even, odd = (total, other) if field % 2 == 0 else (other, total)
                        tile_even = jnp.where(row_number == field, even, tile_even)
                        tile_odd = jnp.where(row_number == field, odd, tile_odd)
                    lanes = pl.ds(pl.multiple_of((2 * step + half) * LANES, LANES), LANES)
                    served[number, 0, :, lanes] = tile_even
                    served[number, 1, :, lanes] = tile_odd
                return carry

            lax.fori_loop(0, slot_rows // 2, look, 0)
            serve(number, FLIPPED[number]).start()
        for number in range(3):
            ask(number, number).wait_send()
            tell_owner(number, number).wait()
            tell_row(number, number).wait()
        for number in range(3):
            serve(number, number).wait_send()
            feed(number).wait_recv()

    @pl.when(side == 1)
    def _():
        load_weight.start()
        load_owner.start()
        rows[...] = jnp.zeros_like(rows)
        load_state.wait()

        def fill(number, carry):
            for level in range(2):
                rows[level * cell_rows + number, 0:fields, :] = state_ref[
                    pl.ds(number * 2 + level, fields, stride=stride), :
                ]
            return carry

        lax.fori_loop(0, cell_rows, fill, 0, unroll=4)
        load_terrain.wait()
        load_weight.wait()
        levels = 2 * groups
        mass = [
            jnp.where((row_number == MASS_ROW) & (level == 2 * group), 1.0, 0.0)
            for level in range(levels)
        ]
        lane_group = (
            lax.broadcasted_iota(jnp.int32, (levels * FIELD_ROWS, LANES), 1) >> 4
        )

        def block_group(number, carry):
            stack = []
            for member in range(8):
                block = number * 8 + member
                lanes = pl.ds(pl.multiple_of(block * LANES, LANES), LANES)
                low = rows[block]
                high = rows[cell_rows + block]
                supply = terrain_ref[:, lanes]
                for level in range(levels):
                    source = jnp.broadcast_to(supply[level : level + 1, :], (FIELD_ROWS, LANES))
                    stack.append(
                        jnp.where(
                            source == 2 * group,
                            low,
                            jnp.where(source == 2 * group + 1, high, 0.0),
                        )
                        + mass[level]
                    )
            values = jnp.concatenate(stack, axis=0)
            coarse_part = values.astype(jnp.bfloat16)
            fine_part = (values - coarse_part.astype(jnp.float32)).astype(jnp.bfloat16)
            left = jnp.concatenate([coarse_part, fine_part], axis=1)
            weight = weight_ref[pl.ds(number * 8, 8)].reshape(8 * 16, LANES)
            weight_high = weight.astype(jnp.bfloat16)
            weight_low = (weight - weight_high.astype(jnp.float32)).astype(jnp.bfloat16)
            right = jnp.concatenate(
                [
                    jnp.concatenate([weight_high, weight_high], axis=1),
                    jnp.concatenate([weight_low, weight_low], axis=1),
                ],
                axis=0,
            )
            product = lax.dot_general(
                left, right, (((1,), (1,)), ((), ())), preferred_element_type=jnp.float32
            )
            total = jnp.zeros((levels * FIELD_ROWS, LANES), jnp.float32)
            for member in range(8):
                span = product[member * levels * FIELD_ROWS : (member + 1) * levels * FIELD_ROWS]
                total = jnp.where(
                    lane_group == member, span[:, :LANES] + span[:, LANES:], total
                )
            lanes = pl.ds(pl.multiple_of(number * LANES, LANES), LANES)
            for level in range(levels):
                part[level // 2, level % 2, :, lanes] = total[
                    level * FIELD_ROWS : (level + 1) * FIELD_ROWS
                ]
            return carry

        lax.fori_loop(0, cell_rows // 8, block_group, 0)
        pl.semaphore_wait(barrier, len(partners) + len(peers))

        def sum_copy(number):
            return remote(
                part.at[peers[number]], sums_in.at[number], sum_send.at[number],
                sum_recv.at[number], place(tile, peers[number], side),
            )

        def merged_copy(number):
            return remote(
                merged, merged_in.at[number], merged_send.at[number],
                merged_recv.at[number], place(tile, peers[number], side),
            )

        def feed(number, slot):
            return remote(
                sums, landed_hbm.at[slot], value_send.at[number],
                value_recv.at[slot], place(partners[number], group, 1 - side),
            )

        def serve(number):
            return remote(
                served.at[number], arrived.at[number], value_send.at[number],
                value_recv.at[number], place(partners[number], group, 1 - side),
            )

        for number in range(len(peers)):
            sum_copy(number).start()
        for number in range(len(peers)):
            sum_copy(number).wait_recv()
        own = part[group]
        for number in range(len(peers)):
            own = own + sums_in[number]
        sums[...] = own
        for number in range(3):
            feed(number, FLIPPED[number]).start()
        load_owner.wait()
        for number in range(3):
            serve(number).wait_recv()
        for slot_row in range(slot_rows):
            lanes = slice(slot_row * LANES, (slot_row + 1) * LANES)
            owner = jnp.broadcast_to(owner_ref[slot_row], (FIELD_ROWS, LANES))
            for level in range(2):
                merged[level, :, lanes] = jnp.where(
                    owner == partners[0],
                    arrived[0, level, :, lanes],
                    jnp.where(
                        owner == partners[1],
                        arrived[1, level, :, lanes],
                        arrived[2, level, :, lanes],
                    ),
                )
        for number in range(len(peers)):
            merged_copy(number).start()
        for number in range(len(peers)):
            merged_copy(number).wait_recv()
        for slot_row in range(slot_rows):
            lanes = slice(slot_row * LANES, (slot_row + 1) * LANES)
            for level in range(2):
                wanted = jnp.broadcast_to(
                    merged[level, fields : fields + 1, lanes], (FIELD_ROWS, LANES)
                )
                value = jnp.zeros((FIELD_ROWS, LANES), jnp.float32)
                for there in range(2):
                    value = jnp.where(
                        wanted == (2 * group + there).astype(jnp.float32),
                        merged[there, :, lanes],
                        value,
                    )
                    for number in range(len(peers)):
                        origin = lax.rem(group + groups - 1 - number, groups)
                        value = jnp.where(
                            wanted == (2 * origin + there).astype(jnp.float32),
                            merged_in[number, there, :, lanes],
                            value,
                        )
                rim_ref[level, :, lanes] = value
        for number in range(len(peers)):
            sum_copy(number).wait_send()
            merged_copy(number).wait_send()
        for number in range(3):
            feed(number, FLIPPED[number]).wait_send()


def finish_kernel(
    sizes, owner_ref, run_ref, state_ref, landed_ref, rim_ref, out_ref, total_low, total_high
):
    fields, cell_rows, slot_rows, blocks = sizes
    tile = lax.axis_index("grid")
    side = lax.axis_index("side")
    stride = 2 * cell_rows
    totals = (total_low, total_high)

    @pl.when(side == 0)
    def _():
        for total in totals:
            total[...] = jnp.zeros_like(total)
        lane_group = lax.broadcasted_iota(jnp.int32, (FIELD_ROWS, LANES), 1) >> 4
        for number in range(3):

            def add(step, carry):
                lanes = pl.ds(pl.multiple_of(step * LANES, LANES), LANES)
                sources = [landed_ref[number, level, :, lanes] for level in range(2)]
                places = []
                moved = []
                for member in range(8):
                    block = step * 8 + member
                    run = run_ref[number, 0, block]
                    target = run & 7
                    shift = ((target - member) & 7) * 16
                    inside = lane_group == target
                    moved.append(
                        [
                            jnp.where(inside, pltpu.roll(source, shift, axis=1), 0.0)
                            for source in sources
                        ]
                    )
                    places.append(
                        jnp.where(owner_ref[number, 0, block] == tile, run >> 3, cell_rows)
                    )
                for member in range(8):
                    for level in range(2):
                        row = places[member]
                        totals[level][row] = totals[level][row] + moved[member][level]
                return carry

            lax.fori_loop(0, blocks // 8, add, 0)

        def close(number, carry):
            mass = total_low[number, MASS_ROW : MASS_ROW + 1, :]
            weight = jnp.broadcast_to(1.0 + mass, (fields, LANES))
            for level in range(2):
                where = pl.ds(number * 2 + level, fields, stride=stride)
                out_ref[where, :] = (
                    state_ref[where, :] + totals[level][number, 0:fields, :]
                ) / weight
            return carry

        lax.fori_loop(0, cell_rows, close, 0, unroll=4)

    @pl.when(side == 1)
    def _():
        out_ref[...] = state_ref[...]
        for number in range(slot_rows):
            for level in range(2):
                where = pl.ds(number * 2 + level, fields, stride=stride)
                out_ref[where, :] = 0.5 * (
                    state_ref[where, :]
                    + rim_ref[level, 0:fields, number * LANES : (number + 1) * LANES]
                )


def on_device(
    tiles, groups,
    model_state, terrain_level, panel_owner, panel_cell, block_weight, block_owner, block_row
):
    _, lev_dev, fields, cells = model_state.shape
    cell_rows = cells // LANES
    slots = panel_cell.shape[0]
    slot_rows = slots // LANES
    blocks = block_row.shape[0]
    state = (
        model_state[0]
        .transpose(1, 0, 2)
        .reshape(fields, lev_dev, cell_rows, LANES)
        .transpose(0, 2, 1, 3)
        .reshape(fields * cell_rows * lev_dev, LANES)
    )
    cell_wanted = panel_cell.reshape(slot_rows, 1, LANES)
    cell_owner = panel_owner.reshape(slot_rows, 1, LANES)
    run_owner = block_owner.reshape(1, blocks)
    run_row = block_row.reshape(1, blocks)
    vmem = pl.BlockSpec(memory_space=pltpu.VMEM)
    smem = pl.BlockSpec(memory_space=pltpu.SMEM)
    hbm = pl.BlockSpec(memory_space=pl.ANY)
    tile_shape = (2, FIELD_ROWS, slots)
    dma = pltpu.SemaphoreType.DMA
    landed, landed_owner, landed_row, rim = pl.pallas_call(
        functools.partial(
            exchange_kernel, (tiles, groups, fields, cell_rows, slot_rows)
        ),
        out_shape=(
            jax.ShapeDtypeStruct((3, *tile_shape), jnp.float32),
            jax.ShapeDtypeStruct((3, 1, blocks), jnp.int32),
            jax.ShapeDtypeStruct((3, 1, blocks), jnp.int32),
            jax.ShapeDtypeStruct(tile_shape, jnp.float32),
        ),
        in_specs=[hbm] * 7,
        out_specs=(hbm, hbm, hbm, vmem),
        scratch_shapes=[
            pltpu.VMEM((slot_rows, 1, LANES), jnp.int32),
            pltpu.VMEM(state.shape, jnp.float32),
            pltpu.VMEM(terrain_level.shape[1:], jnp.int32),
            pltpu.VMEM(block_weight.shape, jnp.float32),
            pltpu.VMEM((2 * cell_rows, FIELD_ROWS, LANES), jnp.float32),
            pltpu.VMEM(((fields + 1) * 2 * cell_rows, 2 * LANES), jnp.bfloat16),
            pltpu.VMEM((2 * cell_rows, LANES), jnp.float32),
            pltpu.VMEM((groups, *tile_shape), jnp.float32),
            pltpu.VMEM((3, *tile_shape), jnp.float32),
            pltpu.VMEM((3, slot_rows, 1, LANES), jnp.int32),
            pltpu.VMEM((3, *tile_shape), jnp.float32),
            pltpu.VMEM(tile_shape, jnp.float32),
            pltpu.VMEM((groups - 1, *tile_shape), jnp.float32),
            pltpu.VMEM(tile_shape, jnp.float32),
            pltpu.VMEM((groups - 1, *tile_shape), jnp.float32),
            dma((4,)),
            *[dma((3,))] * 8,
            *[dma((groups - 1,))] * 4,
        ],
        compiler_params=pltpu.CompilerParams(collective_id=0, has_side_effects=True),
    )(cell_wanted, cell_owner, run_owner, run_row, state, terrain_level[0], block_weight)
    out = pl.pallas_call(
        functools.partial(finish_kernel, (fields, cell_rows, slot_rows, blocks)),
        out_shape=jax.ShapeDtypeStruct(state.shape, jnp.float32),
        in_specs=[smem, smem, vmem, vmem, vmem],
        out_specs=vmem,
        scratch_shapes=[pltpu.VMEM((cell_rows + 1, FIELD_ROWS, LANES), jnp.float32)] * 2,
    )(landed_owner, landed_row, state, landed, rim)
    out = (
        out.reshape(fields, cell_rows, lev_dev, LANES)
        .transpose(0, 2, 1, 3)
        .reshape(fields, lev_dev, cells)
        .transpose(1, 0, 2)
    )
    return out[None]


def solution(mesh):
    in_specs = (
        P("side", "lev", None, "grid"),
        P("side", None, "grid"),
        P("grid", None),
        P("grid"),
        P("grid", None, None),
        P("grid", None),
        P("grid"),
    )
    out_specs = P("side", "lev", None, "grid")
    return jax.shard_map(
        functools.partial(on_device, mesh.shape["grid"], mesh.shape["lev"]),
        mesh=mesh,
        in_specs=in_specs,
        out_specs=out_specs,
        check_vma=False,
    )
```

```python
import functools

import jax
import jax.numpy as jnp
from jax import lax
from jax.experimental import pallas as pl
from jax.experimental.pallas import tpu as pltpu
from jax.sharding import PartitionSpec as P

MESH = pl.DeviceIdType.MESH
LANES = 128
FIELD_ROWS = 8
MASS_ROW = 6
FLIPPED = (1, 0, 2)


def place(grid, lev, side):
    return {"grid": grid, "lev": lev, "side": side}


def exchange_kernel(
    sizes,
    cell_hbm,
    owner_hbm,
    block_owner_hbm,
    block_row_hbm,
    state_hbm,
    terrain_hbm,
    weight_hbm,
    landed_hbm,
    landed_owner_hbm,
    landed_row_hbm,
    rim_ref,
    owner_ref,
    state_ref,
    terrain_ref,
    weight_ref,
    rows,
    table,
    supply_rows,
    part,
    served,
    asked,
    arrived,
    sums,
    sums_in,
    merged,
    merged_in,
    load_sem,
    ask_send,
    ask_recv,
    owner_send,
    owner_recv,
    row_send,
    row_recv,
    value_send,
    value_recv,
    feed_send,
    feed_recv,
    sum_send,
    sum_recv,
    merged_send,
    merged_recv,
):
    tiles, groups, fields, cell_rows, slot_rows = sizes
    tile = lax.axis_index("grid")
    group = lax.axis_index("lev")
    side = lax.axis_index("side")
    partners = [
        lax.rem(tile + step, tiles) for step in (tiles - 1, 1, tiles // 2)
    ]
    peers = [lax.rem(group + step, groups) for step in range(1, groups)]
    steps = slot_rows // 2
    stride = 2 * cell_rows
    span = fields * stride

    barrier = pltpu.get_barrier_semaphore()
    for partner in partners:
        pl.semaphore_signal(
            barrier, inc=1, device_id=place(partner, group, 1 - side), device_id_type=MESH
        )

    @pl.when(side == 0)
    def _():
        for partner in partners:
            pl.semaphore_signal(
                barrier, inc=1, device_id=place(partner, group, side), device_id_type=MESH
            )

    @pl.when(side == 1)
    def _():
        for peer in peers:
            pl.semaphore_signal(
                barrier, inc=1, device_id=place(tile, peer, side), device_id_type=MESH
            )

    load_state = pltpu.make_async_copy(state_hbm, state_ref, load_sem.at[0])
    load_terrain = pltpu.make_async_copy(terrain_hbm, terrain_ref, load_sem.at[1])
    load_weight = pltpu.make_async_copy(weight_hbm, weight_ref, load_sem.at[2])
    load_owner = pltpu.make_async_copy(owner_hbm, owner_ref, load_sem.at[3])
    load_state.start()
    load_terrain.start()

    def remote(source, target, sent, received, where):
        return pltpu.make_async_remote_copy(
            src_ref=source,
            dst_ref=target,
            send_sem=sent,
            recv_sem=received,
            device_id=where,
            device_id_type=MESH,
        )

    row_number = lax.broadcasted_iota(jnp.int32, (FIELD_ROWS, LANES), 0)

    @pl.when(side == 0)
    def _():
        def ask(number, slot):
            return remote(
                cell_hbm, asked.at[slot], ask_send.at[number], ask_recv.at[slot],
                place(partners[number], group, side),
            )

        def tell_owner(number, slot):
            return remote(
                block_owner_hbm, landed_owner_hbm.at[slot], owner_send.at[number],
                owner_recv.at[slot], place(partners[number], group, side),
            )

        def tell_row(number, slot):
            return remote(
                block_row_hbm, landed_row_hbm.at[slot], row_send.at[number],
                row_recv.at[slot], place(partners[number], group, side),
            )

        def serve(number, slot, step):
            return remote(
                served.at[number, step], arrived.at[slot, step], value_send.at[number, step],
                value_recv.at[slot, step], place(partners[number], group, 1 - side),
            )

        def feed(number):
            return remote(
                sums, landed_hbm.at[number], feed_send.at[number],
                feed_recv.at[number], place(partners[number], group, 1 - side),
            )

        pl.semaphore_wait(barrier, len(partners) * 2)
        for number in range(3):
            ask(number, FLIPPED[number]).start()
        for number in range(3):
            tell_owner(number, FLIPPED[number]).start()
            tell_row(number, FLIPPED[number]).start()
        load_terrain.wait()

        def fill(number, carry):
            mixed = jnp.zeros((FIELD_ROWS, LANES), jnp.float32)
            for member in range(4):
                lanes = pl.ds(pl.multiple_of((number * 4 + member) * LANES, LANES), LANES)
                turned = pltpu.roll(
                    terrain_ref[:, lanes].astype(jnp.float32),
                    lax.rem(2 * member + FIELD_ROWS - 2 * group, FIELD_ROWS),
                    axis=0,
                )
                mixed = jnp.where(row_number >> 1 == member, turned, mixed)
            supply_rows[pl.ds(pl.multiple_of(number * FIELD_ROWS, FIELD_ROWS), FIELD_ROWS), :] = (
                mixed
            )
            return carry

        lax.fori_loop(0, cell_rows // 4, fill, 0)
        load_state.wait()

        def split(number, carry):
            where = pl.ds(pl.multiple_of(number * stride, stride), stride)
            value = state_ref[where, :]
            high = value.astype(jnp.bfloat16)
            table[where, :LANES] = high
            table[where, LANES:] = (value - high.astype(jnp.float32)).astype(jnp.bfloat16)
            return carry

        lax.fori_loop(0, fields, split, 0)
        table[span:, :LANES] = supply_rows[...].astype(jnp.bfloat16)
        table[span:, LANES:] = jnp.zeros((stride, LANES), jnp.bfloat16)

        lane_number = lax.broadcasted_iota(jnp.int32, (LANES, LANES), 0)
        row_pair = lax.broadcasted_iota(jnp.int32, (stride, LANES), 0) >> 1
        for number in (1, 0, 2):
            ask(number, number).wait_recv()

            def look(step, carry):
                ones = []
                masks = []
                for half in range(2):
                    wanted = asked[number, 2 * step + half]
                    ones.append(
                        jnp.where(
                            lane_number
                            == jnp.broadcast_to(wanted & (LANES - 1), (LANES, LANES)),
                            1.0,
                            0.0,
                        ).astype(jnp.bfloat16)
                    )
                    masks.append(row_pair == jnp.broadcast_to(wanted >> 7, (stride, LANES)))
                one_hot = jnp.concatenate(ones, axis=1)
                one_hot = jnp.concatenate([one_hot, one_hot], axis=0)
                found = jnp.dot(table[...], one_hot, preferred_element_type=jnp.float32)
                for half in range(2):
                    tile_even = jnp.zeros((FIELD_ROWS, LANES), jnp.float32)
                    tile_odd = tile_even
                    for field in range(fields + 1):
                        picked = jnp.where(
                            masks[half],
                            found[
                                field * stride : (field + 1) * stride,
                                half * LANES : (half + 1) * LANES,
                            ],
                            0.0,
                        )
                        total = jnp.sum(
                            picked.reshape(stride // FIELD_ROWS, FIELD_ROWS, LANES), axis=0
                        )
                        total = total + pltpu.roll(total, 4, axis=0)
                        total = total + pltpu.roll(total, 2, axis=0)
                        other = pltpu.roll(total, 1, axis=0)
                        even, odd = (total, other) if field % 2 == 0 else (other, total)
                        tile_even = jnp.where(row_number == field, even, tile_even)
                        tile_odd = jnp.where(row_number == field, odd, tile_odd)
                    lanes = slice(half * LANES, (half + 1) * LANES)
                    served[number, step, 0, :, lanes] = tile_even
                    served[number, step, 1, :, lanes] = tile_odd
                serve(number, FLIPPED[number], step).start()
                return carry

            lax.fori_loop(0, steps, look, 0)
        for number in range(3):
            ask(number, number).wait_send()
            tell_owner(number, number).wait()
            tell_row(number, number).wait()
        for number in range(3):
            for step in range(steps):
                serve(number, number, step).wait_send()
            feed(number).wait_recv()

    @pl.when(side == 1)
    def _():
        load_weight.start()
        load_owner.start()
        rows[...] = jnp.zeros_like(rows)
        load_state.wait()

        def fill(number, carry):
            for level in range(2):
                rows[level * cell_rows + number, 0:fields, :] = state_ref[
                    pl.ds(number * 2 + level, fields, stride=stride), :
                ]
            return carry

        lax.fori_loop(0, cell_rows, fill, 0, unroll=4)
        load_terrain.wait()
        load_weight.wait()
        levels = 2 * groups
        mass = [
            jnp.where((row_number == MASS_ROW) & (level == 2 * group), 1.0, 0.0)
            for level in range(levels)
        ]
        lane_group = (
            lax.broadcasted_iota(jnp.int32, (levels * FIELD_ROWS, LANES), 1) >> 4
        )

        def block_group(number, carry):
            stack = []
            for member in range(8):
                block = number * 8 + member
                lanes = pl.ds(pl.multiple_of(block * LANES, LANES), LANES)
                low = rows[block]
                high = rows[cell_rows + block]
                supply = terrain_ref[:, lanes]
                for level in range(levels):
                    source = jnp.broadcast_to(supply[level : level + 1, :], (FIELD_ROWS, LANES))
                    stack.append(
                        jnp.where(
                            source == 2 * group,
                            low,
                            jnp.where(source == 2 * group + 1, high, 0.0),
                        )
                        + mass[level]
                    )
            values = jnp.concatenate(stack, axis=0)
            coarse_part = values.astype(jnp.bfloat16)
            fine_part = (values - coarse_part.astype(jnp.float32)).astype(jnp.bfloat16)
            left = jnp.concatenate([coarse_part, fine_part], axis=1)
            weight = weight_ref[pl.ds(number * 8, 8)].reshape(8 * 16, LANES)
            weight_high = weight.astype(jnp.bfloat16)
            weight_low = (weight - weight_high.astype(jnp.float32)).astype(jnp.bfloat16)
            right = jnp.concatenate(
                [
                    jnp.concatenate([weight_high, weight_high], axis=1),
                    jnp.concatenate([weight_low, weight_low], axis=1),
                ],
                axis=0,
            )
            product = lax.dot_general(
                left, right, (((1,), (1,)), ((), ())), preferred_element_type=jnp.float32
            )
            total = jnp.zeros((levels * FIELD_ROWS, LANES), jnp.float32)
            for member in range(8):
                span = product[member * levels * FIELD_ROWS : (member + 1) * levels * FIELD_ROWS]
                total = jnp.where(
                    lane_group == member, span[:, :LANES] + span[:, LANES:], total
                )
            lanes = pl.ds(pl.multiple_of(number * LANES, LANES), LANES)
            for level in range(levels):
                part[level // 2, level % 2, :, lanes] = total[
                    level * FIELD_ROWS : (level + 1) * FIELD_ROWS
                ]
            return carry

        lax.fori_loop(0, cell_rows // 8, block_group, 0)
        pl.semaphore_wait(barrier, len(partners) + len(peers))

        def sum_copy(number):
            return remote(
                part.at[peers[number]], sums_in.at[number], sum_send.at[number],
                sum_recv.at[number], place(tile, peers[number], side),
            )

        def merged_copy(number, step):
            return remote(
                merged.at[step], merged_in.at[number, step], merged_send.at[number, step],
                merged_recv.at[number, step], place(tile, peers[number], side),
            )

        def feed(number, slot):
            return remote(
                sums, landed_hbm.at[slot], feed_send.at[number],
                feed_recv.at[slot], place(partners[number], group, 1 - side),
            )

        def serve(number, step):
            return remote(
                served.at[number, step], arrived.at[number, step], value_send.at[number, step],
                value_recv.at[number, step], place(partners[number], group, 1 - side),
            )

        for number in range(len(peers)):
            sum_copy(number).start()
        for number in range(len(peers)):
            sum_copy(number).wait_recv()
        own = part[group]
        for number in range(len(peers)):
            own = own + sums_in[number]
        sums[...] = own
        for number in range(3):
            feed(number, FLIPPED[number]).start()
        load_owner.wait()
        for step in range(steps):
            for number in range(3):
                serve(number, step).wait_recv()
            for half in range(2):
                lanes = slice(half * LANES, (half + 1) * LANES)
                owner = jnp.broadcast_to(owner_ref[2 * step + half], (FIELD_ROWS, LANES))
                for level in range(2):
                    merged[step, level, :, lanes] = jnp.where(
                        owner == partners[0],
                        arrived[0, step, level, :, lanes],
                        jnp.where(
                            owner == partners[1],
                            arrived[1, step, level, :, lanes],
                            arrived[2, step, level, :, lanes],
                        ),
                    )
            for number in range(len(peers)):
                merged_copy(number, step).start()
        for step in range(steps):
            for number in range(len(peers)):
                merged_copy(number, step).wait_recv()
            for half in range(2):
                lanes = slice(half * LANES, (half + 1) * LANES)
                slot_lanes = slice((2 * step + half) * LANES, (2 * step + half + 1) * LANES)
                for level in range(2):
                    wanted = jnp.broadcast_to(
                        merged[step, level, fields : fields + 1, lanes], (FIELD_ROWS, LANES)
                    )
                    value = jnp.zeros((FIELD_ROWS, LANES), jnp.float32)
                    for there in range(2):
                        value = jnp.where(
                            wanted == (2 * group + there).astype(jnp.float32),
                            merged[step, there, :, lanes],
                            value,
                        )
                        for number in range(len(peers)):
                            origin = lax.rem(group + groups - 1 - number, groups)
                            value = jnp.where(
                                wanted == (2 * origin + there).astype(jnp.float32),
                                merged_in[number, step, there, :, lanes],
                                value,
                            )
                    rim_ref[level, :, slot_lanes] = value
        for number in range(len(peers)):
            sum_copy(number).wait_send()
            for step in range(steps):
                merged_copy(number, step).wait_send()
        for number in range(3):
            feed(number, FLIPPED[number]).wait_send()


def finish_kernel(
    sizes, owner_ref, run_ref, state_ref, landed_ref, rim_ref, out_ref, total_low, total_high
):
    fields, cell_rows, slot_rows, blocks = sizes
    tile = lax.axis_index("grid")
    side = lax.axis_index("side")
    stride = 2 * cell_rows
    totals = (total_low, total_high)

    @pl.when(side == 0)
    def _():
        for total in totals:
            total[...] = jnp.zeros_like(total)
        lane_group = lax.broadcasted_iota(jnp.int32, (FIELD_ROWS, LANES), 1) >> 4
        for number in range(3):

            def add(step, carry):
                lanes = pl.ds(pl.multiple_of(step * LANES, LANES), LANES)
                sources = [landed_ref[number, level, :, lanes] for level in range(2)]
                places = []
                moved = []
                for member in range(8):
                    block = step * 8 + member
                    run = run_ref[number, 0, block]
                    target = run & 7
                    shift = ((target - member) & 7) * 16
                    inside = lane_group == target
                    moved.append(
                        [
                            jnp.where(inside, pltpu.roll(source, shift, axis=1), 0.0)
                            for source in sources
                        ]
                    )
                    places.append(
                        jnp.where(owner_ref[number, 0, block] == tile, run >> 3, cell_rows)
                    )
                for member in range(8):
                    for level in range(2):
                        row = places[member]
                        totals[level][row] = totals[level][row] + moved[member][level]
                return carry

            lax.fori_loop(0, blocks // 8, add, 0)

        def close(number, carry):
            mass = total_low[number, MASS_ROW : MASS_ROW + 1, :]
            weight = jnp.broadcast_to(1.0 + mass, (fields, LANES))
            for level in range(2):
                where = pl.ds(number * 2 + level, fields, stride=stride)
                out_ref[where, :] = (
                    state_ref[where, :] + totals[level][number, 0:fields, :]
                ) / weight
            return carry

        lax.fori_loop(0, cell_rows, close, 0, unroll=4)

    @pl.when(side == 1)
    def _():
        out_ref[...] = state_ref[...]
        for number in range(slot_rows):
            for level in range(2):
                where = pl.ds(number * 2 + level, fields, stride=stride)
                out_ref[where, :] = 0.5 * (
                    state_ref[where, :]
                    + rim_ref[level, 0:fields, number * LANES : (number + 1) * LANES]
                )


def on_device(
    tiles, groups,
    model_state, terrain_level, panel_owner, panel_cell, block_weight, block_owner, block_row
):
    _, lev_dev, fields, cells = model_state.shape
    cell_rows = cells // LANES
    slots = panel_cell.shape[0]
    slot_rows = slots // LANES
    blocks = block_row.shape[0]
    state = (
        model_state[0]
        .transpose(1, 0, 2)
        .reshape(fields, lev_dev, cell_rows, LANES)
        .transpose(0, 2, 1, 3)
        .reshape(fields * cell_rows * lev_dev, LANES)
    )
    cell_wanted = panel_cell.reshape(slot_rows, 1, LANES)
    cell_owner = panel_owner.reshape(slot_rows, 1, LANES)
    run_owner = block_owner.reshape(1, blocks)
    run_row = block_row.reshape(1, blocks)
    vmem = pl.BlockSpec(memory_space=pltpu.VMEM)
    smem = pl.BlockSpec(memory_space=pltpu.SMEM)
    hbm = pl.BlockSpec(memory_space=pl.ANY)
    tile_shape = (2, FIELD_ROWS, slots)
    steps = slot_rows // 2
    chunks = (steps, 2, FIELD_ROWS, 2 * LANES)
    dma = pltpu.SemaphoreType.DMA
    landed, landed_owner, landed_row, rim = pl.pallas_call(
        functools.partial(
            exchange_kernel, (tiles, groups, fields, cell_rows, slot_rows)
        ),
        out_shape=(
            jax.ShapeDtypeStruct((3, *tile_shape), jnp.float32),
            jax.ShapeDtypeStruct((3, 1, blocks), jnp.int32),
            jax.ShapeDtypeStruct((3, 1, blocks), jnp.int32),
            jax.ShapeDtypeStruct(tile_shape, jnp.float32),
        ),
        in_specs=[hbm] * 7,
        out_specs=(hbm, hbm, hbm, vmem),
        scratch_shapes=[
            pltpu.VMEM((slot_rows, 1, LANES), jnp.int32),
            pltpu.VMEM(state.shape, jnp.float32),
            pltpu.VMEM(terrain_level.shape[1:], jnp.int32),
            pltpu.VMEM(block_weight.shape, jnp.float32),
            pltpu.VMEM((2 * cell_rows, FIELD_ROWS, LANES), jnp.float32),
            pltpu.VMEM(((fields + 1) * 2 * cell_rows, 2 * LANES), jnp.bfloat16),
            pltpu.VMEM((2 * cell_rows, LANES), jnp.float32),
            pltpu.VMEM((groups, *tile_shape), jnp.float32),
            pltpu.VMEM((3, *chunks), jnp.float32),
            pltpu.VMEM((3, slot_rows, 1, LANES), jnp.int32),
            pltpu.VMEM((3, *chunks), jnp.float32),
            pltpu.VMEM(tile_shape, jnp.float32),
            pltpu.VMEM((groups - 1, *tile_shape), jnp.float32),
            pltpu.VMEM(chunks, jnp.float32),
            pltpu.VMEM((groups - 1, *chunks), jnp.float32),
            dma((4,)),
            *[dma((3,))] * 6,
            *[dma((3, steps))] * 2,
            *[dma((3,))] * 2,
            *[dma((groups - 1,))] * 2,
            *[dma((groups - 1, steps))] * 2,
        ],
        compiler_params=pltpu.CompilerParams(collective_id=0, has_side_effects=True),
    )(cell_wanted, cell_owner, run_owner, run_row, state, terrain_level[0], block_weight)
    out = pl.pallas_call(
        functools.partial(finish_kernel, (fields, cell_rows, slot_rows, blocks)),
        out_shape=jax.ShapeDtypeStruct(state.shape, jnp.float32),
        in_specs=[smem, smem, vmem, vmem, vmem],
        out_specs=vmem,
        scratch_shapes=[pltpu.VMEM((cell_rows + 1, FIELD_ROWS, LANES), jnp.float32)] * 2,
    )(landed_owner, landed_row, state, landed, rim)
    out = (
        out.reshape(fields, cell_rows, lev_dev, LANES)
        .transpose(0, 2, 1, 3)
        .reshape(fields, lev_dev, cells)
        .transpose(1, 0, 2)
    )
    return out[None]


def solution(mesh):
    in_specs = (
        P("side", "lev", None, "grid"),
        P("side", None, "grid"),
        P("grid", None),
        P("grid"),
        P("grid", None, None),
        P("grid", None),
        P("grid"),
    )
    out_specs = P("side", "lev", None, "grid")
    return jax.shard_map(
        functools.partial(on_device, mesh.shape["grid"], mesh.shape["lev"]),
        mesh=mesh,
        in_specs=in_specs,
        out_specs=out_specs,
        check_vma=False,
    )
```

```python
import functools

import jax
import jax.numpy as jnp
from jax import lax
from jax.experimental import pallas as pl
from jax.experimental.pallas import tpu as pltpu
from jax.sharding import PartitionSpec as P

MESH = pl.DeviceIdType.MESH
LANES = 128
FIELD_ROWS = 8
MASS_ROW = 6
FLIPPED = (1, 0, 2)


def place(grid, lev, side):
    return {"grid": grid, "lev": lev, "side": side}


def exchange_kernel(
    sizes,
    cell_hbm,
    owner_hbm,
    block_owner_hbm,
    block_row_hbm,
    state_hbm,
    terrain_hbm,
    weight_hbm,
    landed_hbm,
    landed_owner_hbm,
    landed_row_hbm,
    rim_ref,
    owner_ref,
    state_ref,
    terrain_ref,
    weight_ref,
    rows,
    table,
    supply_rows,
    part,
    served,
    asked,
    arrived,
    sums,
    sums_in,
    merged,
    merged_in,
    load_sem,
    ask_send,
    ask_recv,
    owner_send,
    owner_recv,
    row_send,
    row_recv,
    value_send,
    value_recv,
    feed_send,
    feed_recv,
    sum_send,
    sum_recv,
    merged_send,
    merged_recv,
):
    tiles, groups, fields, cell_rows, slot_rows = sizes
    tile = lax.axis_index("grid")
    group = lax.axis_index("lev")
    side = lax.axis_index("side")
    partners = [
        lax.rem(tile + step, tiles) for step in (tiles - 1, 1, tiles // 2)
    ]
    peers = [lax.rem(group + step, groups) for step in range(1, groups)]
    steps = slot_rows // 2
    stride = 2 * cell_rows
    span = fields * stride

    barrier = pltpu.get_barrier_semaphore()
    for partner in partners:
        pl.semaphore_signal(
            barrier, inc=1, device_id=place(partner, group, 1 - side), device_id_type=MESH
        )

    @pl.when(side == 0)
    def _():
        for partner in partners:
            pl.semaphore_signal(
                barrier, inc=1, device_id=place(partner, group, side), device_id_type=MESH
            )

    @pl.when(side == 1)
    def _():
        for peer in peers:
            pl.semaphore_signal(
                barrier, inc=1, device_id=place(tile, peer, side), device_id_type=MESH
            )

    load_state = pltpu.make_async_copy(state_hbm, state_ref, load_sem.at[0])
    load_terrain = pltpu.make_async_copy(terrain_hbm, terrain_ref, load_sem.at[1])
    load_weight = pltpu.make_async_copy(weight_hbm, weight_ref, load_sem.at[2])
    load_owner = pltpu.make_async_copy(owner_hbm, owner_ref, load_sem.at[3])
    load_state.start()
    load_terrain.start()

    def remote(source, target, sent, received, where):
        return pltpu.make_async_remote_copy(
            src_ref=source,
            dst_ref=target,
            send_sem=sent,
            recv_sem=received,
            device_id=where,
            device_id_type=MESH,
        )

    row_number = lax.broadcasted_iota(jnp.int32, (FIELD_ROWS, LANES), 0)

    @pl.when(side == 0)
    def _():
        def ask(number, slot):
            return remote(
                cell_hbm, asked.at[slot], ask_send.at[number], ask_recv.at[slot],
                place(partners[number], group, side),
            )

        def tell_owner(number, slot):
            return remote(
                block_owner_hbm, landed_owner_hbm.at[slot], owner_send.at[number],
                owner_recv.at[slot], place(partners[number], group, side),
            )

        def tell_row(number, slot):
            return remote(
                block_row_hbm, landed_row_hbm.at[slot], row_send.at[number],
                row_recv.at[slot], place(partners[number], group, side),
            )

        def serve(number, slot, step):
            return remote(
                served.at[number, step], arrived.at[slot, step], value_send.at[number, step],
                value_recv.at[slot, step], place(partners[number], group, 1 - side),
            )

        def feed(number):
            return remote(
                sums, landed_hbm.at[number], feed_send.at[number],
                feed_recv.at[number], place(partners[number], group, 1 - side),
            )

        pl.semaphore_wait(barrier, len(partners) * 2)
        for number in range(3):
            ask(number, FLIPPED[number]).start()
        for number in range(3):
            tell_owner(number, FLIPPED[number]).start()
            tell_row(number, FLIPPED[number]).start()
        load_terrain.wait()

        def fill(number, carry):
            mixed = jnp.zeros((FIELD_ROWS, LANES), jnp.float32)
            for member in range(4):
                lanes = pl.ds(pl.multiple_of((number * 4 + member) * LANES, LANES), LANES)
                turned = pltpu.roll(
                    terrain_ref[:, lanes].astype(jnp.float32),
                    lax.rem(2 * member + FIELD_ROWS - 2 * group, FIELD_ROWS),
                    axis=0,
                )
                mixed = jnp.where(row_number >> 1 == member, turned, mixed)
            supply_rows[pl.ds(pl.multiple_of(number * FIELD_ROWS, FIELD_ROWS), FIELD_ROWS), :] = (
                mixed
            )
            return carry

        lax.fori_loop(0, cell_rows // 4, fill, 0)
        load_state.wait()

        def split(number, carry):
            where = pl.ds(pl.multiple_of(number * stride, stride), stride)
            value = state_ref[where, :]
            high = value.astype(jnp.bfloat16)
            table[where, :LANES] = high
            table[where, LANES:] = (value - high.astype(jnp.float32)).astype(jnp.bfloat16)
            return carry

        lax.fori_loop(0, fields, split, 0)
        table[span:, :LANES] = supply_rows[...].astype(jnp.bfloat16)
        table[span:, LANES:] = jnp.zeros((stride, LANES), jnp.bfloat16)

        lane_number = lax.broadcasted_iota(jnp.int32, (LANES, LANES), 0)
        row_pair = lax.broadcasted_iota(jnp.int32, (stride, LANES), 0) >> 1
        for number in (1, 0, 2):
            ask(number, number).wait_recv()

            def look(step, carry):
                ones = []
                masks = []
                for half in range(2):
                    wanted = asked[number, 2 * step + half]
                    ones.append(
                        jnp.where(
                            lane_number
                            == jnp.broadcast_to(wanted & (LANES - 1), (LANES, LANES)),
                            1.0,
                            0.0,
                        ).astype(jnp.bfloat16)
                    )
                    masks.append(row_pair == jnp.broadcast_to(wanted >> 7, (stride, LANES)))
                one_hot = jnp.concatenate(ones, axis=1)
                one_hot = jnp.concatenate([one_hot, one_hot], axis=0)
                found = jnp.dot(table[...], one_hot, preferred_element_type=jnp.float32)
                for half in range(2):
                    tile_even = jnp.zeros((FIELD_ROWS, LANES), jnp.float32)
                    tile_odd = tile_even
                    for field in range(fields + 1):
                        picked = jnp.where(
                            masks[half],
                            found[
                                field * stride : (field + 1) * stride,
                                half * LANES : (half + 1) * LANES,
                            ],
                            0.0,
                        )
                        total = jnp.sum(
                            picked.reshape(stride // FIELD_ROWS, FIELD_ROWS, LANES), axis=0
                        )
                        total = total + pltpu.roll(total, 4, axis=0)
                        total = total + pltpu.roll(total, 2, axis=0)
                        other = pltpu.roll(total, 1, axis=0)
                        even, odd = (total, other) if field % 2 == 0 else (other, total)
                        tile_even = jnp.where(row_number == field, even, tile_even)
                        tile_odd = jnp.where(row_number == field, odd, tile_odd)
                    lanes = slice(half * LANES, (half + 1) * LANES)
                    served[number, step, 0, :, lanes] = tile_even
                    served[number, step, 1, :, lanes] = tile_odd
                serve(number, FLIPPED[number], step).start()
                return carry

            lax.fori_loop(0, steps, look, 0)
        for number in range(3):
            ask(number, number).wait_send()
            tell_owner(number, number).wait()
            tell_row(number, number).wait()
        for number in range(3):
            for step in range(steps):
                serve(number, number, step).wait_send()
            feed(number).wait_recv()

    @pl.when(side == 1)
    def _():
        load_weight.start()
        load_owner.start()
        rows[...] = jnp.zeros_like(rows)
        load_state.wait()

        def fill(number, carry):
            for level in range(2):
                rows[level * cell_rows + number, 0:fields, :] = state_ref[
                    pl.ds(number * 2 + level, fields, stride=stride), :
                ]
            return carry

        lax.fori_loop(0, cell_rows, fill, 0, unroll=4)
        load_terrain.wait()
        load_weight.wait()
        levels = 2 * groups
        mass = [
            jnp.where((row_number == MASS_ROW) & (level == 2 * group), 1.0, 0.0)
            for level in range(levels)
        ]
        lane_group = (
            lax.broadcasted_iota(jnp.int32, (levels * FIELD_ROWS, LANES), 1) >> 4
        )

        def block_group(number, carry):
            stack = []
            for member in range(8):
                block = number * 8 + member
                lanes = pl.ds(pl.multiple_of(block * LANES, LANES), LANES)
                low = rows[block]
                high = rows[cell_rows + block]
                supply = terrain_ref[:, lanes]
                for level in range(levels):
                    source = jnp.broadcast_to(supply[level : level + 1, :], (FIELD_ROWS, LANES))
                    stack.append(
                        jnp.where(
                            source == 2 * group,
                            low,
                            jnp.where(source == 2 * group + 1, high, 0.0),
                        )
                        + mass[level]
                    )
            values = jnp.concatenate(stack, axis=0)
            coarse_part = values.astype(jnp.bfloat16)
            fine_part = (values - coarse_part.astype(jnp.float32)).astype(jnp.bfloat16)
            left = jnp.concatenate([coarse_part, fine_part], axis=1)
            weight = weight_ref[pl.ds(number * 8, 8)].reshape(8 * 16, LANES)
            weight_high = weight.astype(jnp.bfloat16)
            weight_low = (weight - weight_high.astype(jnp.float32)).astype(jnp.bfloat16)
            right = jnp.concatenate(
                [
                    jnp.concatenate([weight_high, weight_high], axis=1),
                    jnp.concatenate([weight_low, weight_low], axis=1),
                ],
                axis=0,
            )
            product = lax.dot_general(
                left, right, (((1,), (1,)), ((), ())), preferred_element_type=jnp.float32
            )
            total = jnp.zeros((levels * FIELD_ROWS, LANES), jnp.float32)
            for member in range(8):
                span = product[member * levels * FIELD_ROWS : (member + 1) * levels * FIELD_ROWS]
                total = jnp.where(
                    lane_group == member, span[:, :LANES] + span[:, LANES:], total
                )
            lanes = pl.ds(pl.multiple_of(number * LANES, LANES), LANES)
            for level in range(levels):
                part[level // 2, level % 2, :, lanes] = total[
                    level * FIELD_ROWS : (level + 1) * FIELD_ROWS
                ]
            return carry

        lax.fori_loop(0, cell_rows // 8, block_group, 0)
        pl.semaphore_wait(barrier, len(partners) + len(peers))

        def sum_copy(number):
            return remote(
                part.at[peers[number]], sums_in.at[number], sum_send.at[number],
                sum_recv.at[number], place(tile, peers[number], side),
            )

        def merged_copy(number, step):
            return remote(
                merged.at[step], merged_in.at[number, step], merged_send.at[number, step],
                merged_recv.at[number, step], place(tile, peers[number], side),
            )

        def feed(number, slot):
            return remote(
                sums, landed_hbm.at[slot], feed_send.at[number],
                feed_recv.at[slot], place(partners[number], group, 1 - side),
            )

        def serve(number, step):
            return remote(
                served.at[number, step], arrived.at[number, step], value_send.at[number, step],
                value_recv.at[number, step], place(partners[number], group, 1 - side),
            )

        for number in range(len(peers)):
            sum_copy(number).start()
        for number in range(len(peers)):
            sum_copy(number).wait_recv()
        own = part[group]
        for number in range(len(peers)):
            own = own + sums_in[number]
        sums[...] = own
        for number in range(3):
            feed(number, FLIPPED[number]).start()
        load_owner.wait()
        for step in range(steps):
            for number in range(3):
                serve(number, step).wait_recv()
            for half in range(2):
                lanes = slice(half * LANES, (half + 1) * LANES)
                owner = jnp.broadcast_to(owner_ref[2 * step + half], (FIELD_ROWS, LANES))
                for level in range(2):
                    merged[step, level, :, lanes] = jnp.where(
                        owner == partners[0],
                        arrived[0, step, level, :, lanes],
                        jnp.where(
                            owner == partners[1],
                            arrived[1, step, level, :, lanes],
                            arrived[2, step, level, :, lanes],
                        ),
                    )
            for number in range(len(peers)):
                merged_copy(number, step).start()
        for step in range(steps):
            for number in range(len(peers)):
                merged_copy(number, step).wait_recv()
            for half in range(2):
                lanes = slice(half * LANES, (half + 1) * LANES)
                slot_lanes = slice((2 * step + half) * LANES, (2 * step + half + 1) * LANES)
                for level in range(2):
                    wanted = jnp.broadcast_to(
                        merged[step, level, fields : fields + 1, lanes], (FIELD_ROWS, LANES)
                    )
                    value = jnp.zeros((FIELD_ROWS, LANES), jnp.float32)
                    for there in range(2):
                        value = jnp.where(
                            wanted == (2 * group + there).astype(jnp.float32),
                            merged[step, there, :, lanes],
                            value,
                        )
                        for number in range(len(peers)):
                            origin = lax.rem(group + groups - 1 - number, groups)
                            value = jnp.where(
                                wanted == (2 * origin + there).astype(jnp.float32),
                                merged_in[number, step, there, :, lanes],
                                value,
                            )
                    rim_ref[level, :, slot_lanes] = value
        for number in range(len(peers)):
            sum_copy(number).wait_send()
            for step in range(steps):
                merged_copy(number, step).wait_send()
        for number in range(3):
            feed(number, FLIPPED[number]).wait_send()


def finish_kernel(
    sizes, owner_ref, run_ref, state_ref, landed_ref, rim_ref, out_ref, total_low, total_high
):
    fields, cell_rows, slot_rows, blocks = sizes
    tile = lax.axis_index("grid")
    side = lax.axis_index("side")
    stride = 2 * cell_rows
    totals = (total_low, total_high)

    @pl.when(side == 0)
    def _():
        for total in totals:
            total[...] = jnp.zeros_like(total)
        lane_group = lax.broadcasted_iota(jnp.int32, (FIELD_ROWS, LANES), 1) >> 4
        for number in range(3):

            def add(step, carry):
                lanes = pl.ds(pl.multiple_of(step * LANES, LANES), LANES)
                sources = [landed_ref[number, level, :, lanes] for level in range(2)]
                places = []
                moved = []
                for member in range(8):
                    block = step * 8 + member
                    run = run_ref[number, 0, block]
                    target = run & 7
                    shift = ((target - member) & 7) * 16
                    inside = lane_group == target
                    moved.append(
                        [
                            jnp.where(inside, pltpu.roll(source, shift, axis=1), 0.0)
                            for source in sources
                        ]
                    )
                    places.append(
                        jnp.where(owner_ref[number, 0, block] == tile, run >> 3, cell_rows)
                    )
                for member in range(8):
                    for level in range(2):
                        row = places[member]
                        totals[level][row] = totals[level][row] + moved[member][level]
                return carry

            lax.fori_loop(0, blocks // 8, add, 0)

        def close(number, carry):
            mass = total_low[number, MASS_ROW : MASS_ROW + 1, :]
            weight = jnp.broadcast_to(1.0 + mass, (fields, LANES))
            for level in range(2):
                where = pl.ds(number * 2 + level, fields, stride=stride)
                out_ref[where, :] = (
                    state_ref[where, :] + totals[level][number, 0:fields, :]
                ) / weight
            return carry

        lax.fori_loop(0, cell_rows, close, 0, unroll=4)

    @pl.when(side == 1)
    def _():
        out_ref[...] = state_ref[...]
        for number in range(slot_rows):
            for level in range(2):
                where = pl.ds(number * 2 + level, fields, stride=stride)
                out_ref[where, :] = 0.5 * (
                    state_ref[where, :]
                    + rim_ref[level, 0:fields, number * LANES : (number + 1) * LANES]
                )


def on_device(
    tiles, groups,
    model_state, terrain_level, panel_owner, panel_cell, block_weight, block_owner, block_row
):
    _, lev_dev, fields, cells = model_state.shape
    cell_rows = cells // LANES
    slots = panel_cell.shape[0]
    slot_rows = slots // LANES
    blocks = block_row.shape[0]
    state = (
        model_state[0]
        .transpose(1, 0, 2)
        .reshape(fields, lev_dev, cell_rows, LANES)
        .transpose(0, 2, 1, 3)
        .reshape(fields * cell_rows * lev_dev, LANES)
    )
    cell_wanted = panel_cell.reshape(slot_rows, 1, LANES)
    cell_owner = panel_owner.reshape(slot_rows, 1, LANES)
    run_owner = block_owner.reshape(1, blocks)
    run_row = block_row.reshape(1, blocks)
    vmem = pl.BlockSpec(memory_space=pltpu.VMEM)
    smem = pl.BlockSpec(memory_space=pltpu.SMEM)
    hbm = pl.BlockSpec(memory_space=pl.ANY)
    tile_shape = (2, FIELD_ROWS, slots)
    steps = slot_rows // 2
    chunks = (steps, 2, FIELD_ROWS, 2 * LANES)
    dma = pltpu.SemaphoreType.DMA
    landed, landed_owner, landed_row, rim = pl.pallas_call(
        functools.partial(
            exchange_kernel, (tiles, groups, fields, cell_rows, slot_rows)
        ),
        out_shape=(
            jax.ShapeDtypeStruct((3, *tile_shape), jnp.float32),
            jax.ShapeDtypeStruct((3, 1, blocks), jnp.int32),
            jax.ShapeDtypeStruct((3, 1, blocks), jnp.int32),
            jax.ShapeDtypeStruct(tile_shape, jnp.float32),
        ),
        in_specs=[hbm] * 7,
        out_specs=(hbm, hbm, hbm, vmem),
        scratch_shapes=[
            pltpu.VMEM((slot_rows, 1, LANES), jnp.int32),
            pltpu.VMEM(state.shape, jnp.float32),
            pltpu.VMEM(terrain_level.shape[1:], jnp.int32),
            pltpu.VMEM(block_weight.shape, jnp.float32),
            pltpu.VMEM((2 * cell_rows, FIELD_ROWS, LANES), jnp.float32),
            pltpu.VMEM(((fields + 1) * 2 * cell_rows, 2 * LANES), jnp.bfloat16),
            pltpu.VMEM((2 * cell_rows, LANES), jnp.float32),
            pltpu.VMEM((groups, *tile_shape), jnp.float32),
            pltpu.VMEM((3, *chunks), jnp.float32),
            pltpu.VMEM((3, slot_rows, 1, LANES), jnp.int32),
            pltpu.VMEM((3, *chunks), jnp.float32),
            pltpu.VMEM(tile_shape, jnp.float32),
            pltpu.VMEM((groups - 1, *tile_shape), jnp.float32),
            pltpu.VMEM(chunks, jnp.float32),
            pltpu.VMEM((groups - 1, *chunks), jnp.float32),
            dma((4,)),
            *[dma((3,))] * 6,
            *[dma((3, steps))] * 2,
            *[dma((3,))] * 2,
            *[dma((groups - 1,))] * 2,
            *[dma((groups - 1, steps))] * 2,
        ],
        compiler_params=pltpu.CompilerParams(collective_id=0, has_side_effects=True, vmem_limit_bytes=16 * 1024 * 1024),
    )(*(pltpu.with_memory_space_constraint(x, pltpu.HBM) for x in (cell_wanted, cell_owner, run_owner, run_row, state, terrain_level[0], block_weight)))
    out = pl.pallas_call(
        functools.partial(finish_kernel, (fields, cell_rows, slot_rows, blocks)),
        out_shape=jax.ShapeDtypeStruct(state.shape, jnp.float32),
        in_specs=[smem, smem, vmem, vmem, vmem],
        out_specs=vmem,
        compiler_params=pltpu.CompilerParams(vmem_limit_bytes=8*1024*1024),
        scratch_shapes=[pltpu.VMEM((cell_rows + 1, FIELD_ROWS, LANES), jnp.float32)] * 2,
    )(landed_owner, landed_row, state, landed, rim)
    out = (
        out.reshape(fields, cell_rows, lev_dev, LANES)
        .transpose(0, 2, 1, 3)
        .reshape(fields, lev_dev, cells)
        .transpose(1, 0, 2)
    )
    return out[None]


def solution(mesh):
    in_specs = (
        P("side", "lev", None, "grid"),
        P("side", None, "grid"),
        P("grid", None),
        P("grid"),
        P("grid", None, None),
        P("grid", None),
        P("grid"),
    )
    out_specs = P("side", "lev", None, "grid")
    return jax.shard_map(
        functools.partial(on_device, mesh.shape["grid"], mesh.shape["lev"]),
        mesh=mesh,
        in_specs=in_specs,
        out_specs=out_specs,
        check_vma=False,
    )
```

```python
import functools

import jax
import jax.numpy as jnp
from jax import lax
from jax.experimental import pallas as pl
from jax.experimental.pallas import tpu as pltpu
from jax.sharding import PartitionSpec as P

MESH = pl.DeviceIdType.MESH
LANES = 128
FIELD_ROWS = 8
MASS_ROW = 6
FLIPPED = (1, 0, 2)
COPIES = 4


def place(grid, lev, side):
    return {"grid": grid, "lev": lev, "side": side}


def exchange_kernel(
    sizes,
    cell_hbm,
    owner_hbm,
    block_owner_hbm,
    block_row_hbm,
    state_hbm,
    terrain_hbm,
    weight_hbm,
    landed_hbm,
    landed_owner_hbm,
    landed_row_hbm,
    rim_ref,
    owner_ref,
    state_ref,
    terrain_ref,
    weight_ref,
    rows,
    table,
    supply_rows,
    part,
    served,
    asked,
    arrived,
    sums,
    sums_in,
    merged,
    merged_in,
    load_sem,
    ask_send,
    ask_recv,
    owner_send,
    owner_recv,
    row_send,
    row_recv,
    value_send,
    value_recv,
    feed_send,
    feed_recv,
    sum_send,
    sum_recv,
    merged_send,
    merged_recv,
):
    tiles, groups, fields, cell_rows, slot_rows = sizes
    tile = lax.axis_index("grid")
    group = lax.axis_index("lev")
    side = lax.axis_index("side")
    partners = [
        lax.rem(tile + step, tiles) for step in (tiles - 1, 1, tiles // 2)
    ]
    peers = [lax.rem(group + step, groups) for step in range(1, groups)]
    steps = slot_rows // 2
    stride = 2 * cell_rows
    span = fields * stride

    barrier = pltpu.get_barrier_semaphore()

    @pl.when(side == 0)
    def _():
        for partner, core in (
            (partners[0], 0), (partners[2], 0), (partners[0], 1), (partners[1], 1), (partners[2], 1)
        ):
            pl.semaphore_signal(
                barrier, inc=1, device_id=place(partner, group, core), device_id_type=MESH
            )

    @pl.when(side == 1)
    def _():
        pl.semaphore_signal(
            barrier, inc=1, device_id=place(tile, group, 0), device_id_type=MESH
        )
        for peer in peers:
            pl.semaphore_signal(
                barrier, inc=1, device_id=place(tile, peer, 1), device_id_type=MESH
            )

    load_state = pltpu.make_async_copy(state_hbm, state_ref, load_sem.at[0])
    load_terrain = pltpu.make_async_copy(terrain_hbm, terrain_ref, load_sem.at[1])
    load_weight = pltpu.make_async_copy(weight_hbm, weight_ref, load_sem.at[2])
    load_owner = pltpu.make_async_copy(owner_hbm, owner_ref, load_sem.at[3])
    load_state.start()
    load_terrain.start()

    def remote(source, target, sent, received, where):
        return pltpu.make_async_remote_copy(
            src_ref=source,
            dst_ref=target,
            send_sem=sent,
            recv_sem=received,
            device_id=where,
            device_id_type=MESH,
        )

    def ask(number, slot):
        return remote(
            cell_hbm, asked.at[slot], ask_send.at[number], ask_recv.at[slot],
            place(partners[number], group, 0),
        )

    def tell_owner(number, slot):
        return remote(
            block_owner_hbm, landed_owner_hbm.at[slot], owner_send.at[number],
            owner_recv.at[slot], place(partners[number], group, 0),
        )

    def tell_row(number, slot):
        return remote(
            block_row_hbm, landed_row_hbm.at[slot], row_send.at[number],
            row_recv.at[slot], place(partners[number], group, 0),
        )

    row_number = lax.broadcasted_iota(jnp.int32, (FIELD_ROWS, LANES), 0)

    @pl.when(side == 0)
    def _():
        def serve(number, slot, step):
            return remote(
                served.at[number, step], arrived.at[slot, step], value_send.at[number, step],
                value_recv.at[slot, step], place(partners[number], group, 1 - side),
            )

        def feed(number, half):
            return remote(
                sums.at[half], landed_hbm.at[number, half], feed_send.at[number, half],
                feed_recv.at[number, half], place(partners[number], group, 1 - side),
            )

        pl.semaphore_wait(barrier, 3)
        for number in (1, 2):
            ask(number, FLIPPED[number]).start()
        for number in (1, 2):
            tell_owner(number, FLIPPED[number]).start()
            tell_row(number, FLIPPED[number]).start()
        load_terrain.wait()

        def fill(number, carry):
            mixed = jnp.zeros((FIELD_ROWS, LANES), jnp.float32)
            for member in range(4):
                lanes = pl.ds(pl.multiple_of((number * 4 + member) * LANES, LANES), LANES)
                turned = pltpu.roll(
                    terrain_ref[:, lanes].astype(jnp.float32),
                    lax.rem(2 * member + FIELD_ROWS - 2 * group, FIELD_ROWS),
                    axis=0,
                )
                mixed = jnp.where(row_number >> 1 == member, turned, mixed)
            supply_rows[pl.ds(pl.multiple_of(number * FIELD_ROWS, FIELD_ROWS), FIELD_ROWS), :] = (
                mixed
            )
            return carry

        lax.fori_loop(0, cell_rows // 4, fill, 0)
        load_state.wait()

        def split(number, carry):
            where = pl.ds(pl.multiple_of(number * stride, stride), stride)
            value = state_ref[where, :]
            high = value.astype(jnp.bfloat16)
            table[where, :LANES] = high
            table[where, LANES:] = (value - high.astype(jnp.float32)).astype(jnp.bfloat16)
            return carry

        lax.fori_loop(0, fields, split, 0)
        table[span:, :LANES] = supply_rows[...].astype(jnp.bfloat16)
        table[span:, LANES:] = jnp.zeros((stride, LANES), jnp.bfloat16)

        lane_number = lax.broadcasted_iota(jnp.int32, (LANES, LANES), 0)
        row_pair = lax.broadcasted_iota(jnp.int32, (stride, LANES), 0) >> 1
        for number in (1, 2, 0):
            ask(number, number).wait_recv()

            def look(step, carry):
                ones = []
                masks = []
                for half in range(2):
                    wanted = asked[number, 2 * step + half]
                    ones.append(
                        jnp.where(
                            lane_number
                            == jnp.broadcast_to(wanted & (LANES - 1), (LANES, LANES)),
                            1.0,
                            0.0,
                        ).astype(jnp.bfloat16)
                    )
                    masks.append(row_pair == jnp.broadcast_to(wanted >> 7, (stride, LANES)))
                one_hot = jnp.concatenate(ones, axis=1)
                one_hot = jnp.concatenate([one_hot, one_hot], axis=0)
                found = jnp.dot(table[...], one_hot, preferred_element_type=jnp.float32)
                for half in range(2):
                    tile_even = jnp.zeros((FIELD_ROWS, LANES), jnp.float32)
                    tile_odd = tile_even
                    for field in range(fields + 1):
                        picked = jnp.where(
                            masks[half],
                            found[
                                field * stride : (field + 1) * stride,
                                half * LANES : (half + 1) * LANES,
                            ],
                            0.0,
                        )
                        total = jnp.sum(
                            picked.reshape(stride // FIELD_ROWS, FIELD_ROWS, LANES), axis=0
                        )
                        total = total + pltpu.roll(total, 4, axis=0)
                        total = total + pltpu.roll(total, 2, axis=0)
                        other = pltpu.roll(total, 1, axis=0)
                        even, odd = (total, other) if field % 2 == 0 else (other, total)
                        tile_even = jnp.where(row_number == field, even, tile_even)
                        tile_odd = jnp.where(row_number == field, odd, tile_odd)
                    lanes = slice(half * LANES, (half + 1) * LANES)
                    served[number, step, 0, :, lanes] = tile_even
                    served[number, step, 1, :, lanes] = tile_odd
                serve(number, FLIPPED[number], step).start()
                return carry

            lax.fori_loop(0, steps, look, 0)
        for number in (1, 2):
            ask(number, number).wait_send()
            tell_owner(number, number).wait_send()
            tell_row(number, number).wait_send()
        for number in range(3):
            tell_owner(number, number).wait_recv()
            tell_row(number, number).wait_recv()
            for step in range(steps):
                serve(number, number, step).wait_send()
        for half in range(2):
            for number in range(3):
                feed(number, half).wait_recv()

    @pl.when(side == 1)
    def _():
        load_weight.start()
        load_owner.start()
        rows[...] = jnp.zeros_like(rows)
        load_state.wait()

        def fill(number, carry):
            for level in range(2):
                rows[level * cell_rows + number, 0:fields, :] = state_ref[
                    pl.ds(number * 2 + level, fields, stride=stride), :
                ]
            return carry

        lax.fori_loop(0, cell_rows, fill, 0, unroll=4)
        load_terrain.wait()
        load_weight.wait()
        levels = 2 * groups
        half_groups = cell_rows // 16
        mass = [
            jnp.where((row_number == MASS_ROW) & (level == 2 * group), 1.0, 0.0)
            for level in range(levels)
        ]
        lane_group = (
            lax.broadcasted_iota(jnp.int32, (levels * FIELD_ROWS, LANES), 1) >> 4
        )

        def block_group(half, step, carry):
            number = half * half_groups + step
            stack = []
            for member in range(8):
                block = number * 8 + member
                lanes = pl.ds(pl.multiple_of(block * LANES, LANES), LANES)
                low = rows[block]
                high = rows[cell_rows + block]
                supply = terrain_ref[:, lanes]
                for level in range(levels):
                    source = jnp.broadcast_to(supply[level : level + 1, :], (FIELD_ROWS, LANES))
                    stack.append(
                        jnp.where(
                            source == 2 * group,
                            low,
                            jnp.where(source == 2 * group + 1, high, 0.0),
                        )
                        + mass[level]
                    )
            values = jnp.concatenate(stack, axis=0)
            coarse_part = values.astype(jnp.bfloat16)
            fine_part = (values - coarse_part.astype(jnp.float32)).astype(jnp.bfloat16)
            left = jnp.concatenate([coarse_part, fine_part], axis=1)
            weight = weight_ref[pl.ds(number * 8, 8)].reshape(8 * 16, LANES)
            weight_high = weight.astype(jnp.bfloat16)
            weight_low = (weight - weight_high.astype(jnp.float32)).astype(jnp.bfloat16)
            right = jnp.concatenate(
                [
                    jnp.concatenate([weight_high, weight_high], axis=1),
                    jnp.concatenate([weight_low, weight_low], axis=1),
                ],
                axis=0,
            )
            product = lax.dot_general(
                left, right, (((1,), (1,)), ((), ())), preferred_element_type=jnp.float32
            )
            total = jnp.zeros((levels * FIELD_ROWS, LANES), jnp.float32)
            for member in range(8):
                span = product[member * levels * FIELD_ROWS : (member + 1) * levels * FIELD_ROWS]
                total = jnp.where(
                    lane_group == member, span[:, :LANES] + span[:, LANES:], total
                )
            lanes = pl.ds(pl.multiple_of(step * LANES, LANES), LANES)
            for level in range(levels):
                part[half, level // 2, level % 2, :, lanes] = total[
                    level * FIELD_ROWS : (level + 1) * FIELD_ROWS
                ]
            return carry

        def sum_copy(number, half):
            return remote(
                part.at[half, peers[number]], sums_in.at[half, number],
                sum_send.at[number, half], sum_recv.at[number, half],
                place(tile, peers[number], side),
            )

        def merged_copy(number, step):
            return remote(
                merged.at[step], merged_in.at[number, step], merged_send.at[number, step],
                merged_recv.at[number, step], place(tile, peers[number], side),
            )

        def feed(number, slot, half):
            return remote(
                sums.at[half], landed_hbm.at[slot, half], feed_send.at[number, half],
                feed_recv.at[slot, half], place(partners[number], group, 1 - side),
            )

        def serve(number, step):
            return remote(
                served.at[number, step], arrived.at[number, step], value_send.at[number, step],
                value_recv.at[number, step], place(partners[number], group, 1 - side),
            )

        lax.fori_loop(0, half_groups, functools.partial(block_group, 0), 0)
        pl.semaphore_wait(barrier, 3 + len(peers))
        ask(0, FLIPPED[0]).start()
        for number in range(len(peers)):
            sum_copy(number, 0).start()
        tell_owner(0, FLIPPED[0]).start()
        tell_row(0, FLIPPED[0]).start()
        lax.fori_loop(0, half_groups, functools.partial(block_group, 1), 0)
        for number in range(len(peers)):
            sum_copy(number, 1).start()
        for half in range(2):
            for number in range(len(peers)):
                sum_copy(number, half).wait_recv()
            own = part[half, group]
            for number in range(len(peers)):
                own = own + sums_in[half, number]
            sums[half] = own
            for number in range(3):
                feed(number, FLIPPED[number], half).start()
        load_owner.wait()
        for step in range(steps):
            for number in range(3):
                serve(number, step).wait_recv()
            for half in range(2):
                lanes = slice(half * LANES, (half + 1) * LANES)
                owner = jnp.broadcast_to(owner_ref[2 * step + half], (FIELD_ROWS, LANES))
                for level in range(2):
                    merged[step, level, :, lanes] = jnp.where(
                        owner == partners[0],
                        arrived[0, step, level, :, lanes],
                        jnp.where(
                            owner == partners[1],
                            arrived[1, step, level, :, lanes],
                            arrived[2, step, level, :, lanes],
                        ),
                    )
            for number in range(len(peers)):
                merged_copy(number, step).start()
        for step in range(steps):
            for number in range(len(peers)):
                merged_copy(number, step).wait_recv()
            for half in range(2):
                lanes = slice(half * LANES, (half + 1) * LANES)
                slot_lanes = slice((2 * step + half) * LANES, (2 * step + half + 1) * LANES)
                for level in range(2):
                    wanted = jnp.broadcast_to(
                        merged[step, level, fields : fields + 1, lanes], (FIELD_ROWS, LANES)
                    )
                    value = jnp.zeros((FIELD_ROWS, LANES), jnp.float32)
                    for there in range(2):
                        value = jnp.where(
                            wanted == (2 * group + there).astype(jnp.float32),
                            merged[step, there, :, lanes],
                            value,
                        )
                        for number in range(len(peers)):
                            origin = lax.rem(group + groups - 1 - number, groups)
                            value = jnp.where(
                                wanted == (2 * origin + there).astype(jnp.float32),
                                merged_in[number, step, there, :, lanes],
                                value,
                            )
                    rim_ref[level, :, slot_lanes] = value
        ask(0, FLIPPED[0]).wait_send()
        tell_owner(0, FLIPPED[0]).wait_send()
        tell_row(0, FLIPPED[0]).wait_send()
        for number in range(len(peers)):
            for half in range(2):
                sum_copy(number, half).wait_send()
            for step in range(steps):
                merged_copy(number, step).wait_send()
        for number in range(3):
            for half in range(2):
                feed(number, FLIPPED[number], half).wait_send()


def finish_kernel(
    sizes, owner_ref, run_ref, state_ref, landed_ref, rim_ref, out_hbm, result, sems, *totals
):
    fields, cell_rows, slot_rows, blocks = sizes
    tile = lax.axis_index("grid")
    side = lax.axis_index("side")
    stride = 2 * cell_rows
    rim_rows = 2 * slot_rows
    half_groups = cell_rows // 16

    def put(source, field, first, count, slot):
        where = pl.ds(field * stride + first, count)
        return pltpu.make_async_copy(source.at[where], out_hbm.at[where], sems.at[slot, field])

    @pl.when(side == 0)
    def _():
        for total in totals:
            total[...] = jnp.zeros_like(total)
        lane_group = lax.broadcasted_iota(jnp.int32, (FIELD_ROWS, LANES), 1) >> 4
        for number in range(3):
            for half in range(2):

                def add(step, carry):
                    lanes = pl.ds(pl.multiple_of(step * LANES, LANES), LANES)
                    sources = [landed_ref[number, half, level, :, lanes] for level in range(2)]
                    places = []
                    moved = []
                    for member in range(8):
                        block = (half * half_groups + step) * 8 + member
                        run = run_ref[number, 0, block]
                        target = run & 7
                        shift = ((target - member) & 7) * 16
                        inside = lane_group == target
                        moved.append(
                            [
                                jnp.where(inside, pltpu.roll(source, shift, axis=1), 0.0)
                                for source in sources
                            ]
                        )
                        row = jnp.where(owner_ref[number, 0, block] == tile, run >> 3, cell_rows)
                        places.append(pl.ds(pl.multiple_of(row * FIELD_ROWS, FIELD_ROWS), FIELD_ROWS))
                    for member in range(8):
                        for level in range(2):
                            total = totals[(member % COPIES) * 2 + level]
                            where = places[member]
                            total[where, :] = total[where, :] + moved[member][level]
                    return carry

                lax.fori_loop(0, half_groups, add, 0)

        def gathered(level, row):
            value = totals[level][pl.ds(row, cell_rows, stride=FIELD_ROWS), :]
            for copy in range(1, COPIES):
                value = value + totals[copy * 2 + level][
                    pl.ds(row, cell_rows, stride=FIELD_ROWS), :
                ]
            return value

        scale = 1.0 / (1.0 + gathered(0, MASS_ROW))
        for field in range(fields):
            for level in range(2):
                where = pl.ds(field * stride + level, cell_rows, stride=2)
                result[where, :] = (state_ref[where, :] + gathered(level, field)) * scale
            put(result, field, 0, stride, 0).start()
        for field in range(fields):
            put(result, field, 0, stride, 0).wait()

    @pl.when(side == 1)
    def _():
        for field in range(fields):
            put(state_ref, field, rim_rows, stride - rim_rows, 0).start()
        for number in range(slot_rows):
            for level in range(2):
                where = pl.ds(number * 2 + level, fields, stride=stride)
                result[where, :] = 0.5 * (
                    state_ref[where, :]
                    + rim_ref[level, 0:fields, number * LANES : (number + 1) * LANES]
                )
        for field in range(fields):
            put(result, field, 0, rim_rows, 1).start()
        for field in range(fields):
            put(state_ref, field, rim_rows, stride - rim_rows, 0).wait()
            put(result, field, 0, rim_rows, 1).wait()


def on_device(
    tiles, groups,
    model_state, terrain_level, panel_owner, panel_cell, block_weight, block_owner, block_row
):
    _, lev_dev, fields, cells = model_state.shape
    cell_rows = cells // LANES
    slots = panel_cell.shape[0]
    slot_rows = slots // LANES
    blocks = block_row.shape[0]
    state = (
        model_state[0]
        .transpose(1, 0, 2)
        .reshape(fields, lev_dev, cell_rows, LANES)
        .transpose(0, 2, 1, 3)
        .reshape(fields * cell_rows * lev_dev, LANES)
    )
    cell_wanted = panel_cell.reshape(slot_rows, 1, LANES)
    cell_owner = panel_owner.reshape(slot_rows, 1, LANES)
    run_owner = block_owner.reshape(1, blocks)
    run_row = block_row.reshape(1, blocks)
    vmem = pl.BlockSpec(memory_space=pltpu.VMEM)
    smem = pl.BlockSpec(memory_space=pltpu.SMEM)
    hbm = pl.BlockSpec(memory_space=pl.ANY)
    tile_shape = (2, FIELD_ROWS, slots)
    steps = slot_rows // 2
    chunks = (steps, 2, FIELD_ROWS, 2 * LANES)
    halves = (2, 2, FIELD_ROWS, blocks * 8)
    dma = pltpu.SemaphoreType.DMA
    landed, landed_owner, landed_row, rim = pl.pallas_call(
        functools.partial(
            exchange_kernel, (tiles, groups, fields, cell_rows, slot_rows)
        ),
        out_shape=(
            jax.ShapeDtypeStruct((3, *halves), jnp.float32),
            jax.ShapeDtypeStruct((3, 1, blocks), jnp.int32),
            jax.ShapeDtypeStruct((3, 1, blocks), jnp.int32),
            jax.ShapeDtypeStruct(tile_shape, jnp.float32),
        ),
        in_specs=[hbm] * 7,
        out_specs=(hbm, hbm, hbm, vmem),
        scratch_shapes=[
            pltpu.VMEM((slot_rows, 1, LANES), jnp.int32),
            pltpu.VMEM(state.shape, jnp.float32),
            pltpu.VMEM(terrain_level.shape[1:], jnp.int32),
            pltpu.VMEM(block_weight.shape, jnp.float32),
            pltpu.VMEM((2 * cell_rows, FIELD_ROWS, LANES), jnp.float32),
            pltpu.VMEM(((fields + 1) * 2 * cell_rows, 2 * LANES), jnp.bfloat16),
            pltpu.VMEM((2 * cell_rows, LANES), jnp.float32),
            pltpu.VMEM((2, groups, *halves[1:]), jnp.float32),
            pltpu.VMEM((3, *chunks), jnp.float32),
            pltpu.VMEM((3, slot_rows, 1, LANES), jnp.int32),
            pltpu.VMEM((3, *chunks), jnp.float32),
            pltpu.VMEM(halves, jnp.float32),
            pltpu.VMEM((2, groups - 1, *halves[1:]), jnp.float32),
            pltpu.VMEM(chunks, jnp.float32),
            pltpu.VMEM((groups - 1, *chunks), jnp.float32),
            dma((4,)),
            *[dma((3,))] * 6,
            *[dma((3, steps))] * 2,
            *[dma((3, 2))] * 2,
            *[dma((groups - 1, 2))] * 2,
            *[dma((groups - 1, steps))] * 2,
        ],
        compiler_params=pltpu.CompilerParams(collective_id=0, has_side_effects=True, vmem_limit_bytes=16 * 1024 * 1024),
    )(*(pltpu.with_memory_space_constraint(x, pltpu.HBM) for x in (cell_wanted, cell_owner, run_owner, run_row, state, terrain_level[0], block_weight)))
    out = pl.pallas_call(
        functools.partial(finish_kernel, (fields, cell_rows, slot_rows, blocks)),
        out_shape=jax.ShapeDtypeStruct(state.shape, jnp.float32),
        in_specs=[smem, smem, vmem, vmem, vmem],
        out_specs=pl.BlockSpec(memory_space=pl.ANY),
        compiler_params=pltpu.CompilerParams(vmem_limit_bytes=8 * 1024 * 1024),
        scratch_shapes=[
            pltpu.VMEM(state.shape, jnp.float32),
            dma((2, fields)),
            *[pltpu.VMEM(((cell_rows + 1) * FIELD_ROWS, LANES), jnp.float32)] * (2 * COPIES),
        ],
    )(landed_owner, landed_row, state, landed, rim)
    out = (
        out.reshape(fields, cell_rows, lev_dev, LANES)
        .transpose(0, 2, 1, 3)
        .reshape(fields, lev_dev, cells)
        .transpose(1, 0, 2)
    )
    return out[None]


def solution(mesh):
    in_specs = (
        P("side", "lev", None, "grid"),
        P("side", None, "grid"),
        P("grid", None),
        P("grid"),
        P("grid", None, None),
        P("grid", None),
        P("grid"),
    )
    out_specs = P("side", "lev", None, "grid")
    return jax.shard_map(
        functools.partial(on_device, mesh.shape["grid"], mesh.shape["lev"]),
        mesh=mesh,
        in_specs=in_specs,
        out_specs=out_specs,
        check_vma=False,
    )
```

```python
import functools

import jax
import jax.numpy as jnp
from jax import lax
from jax.experimental import pallas as pl
from jax.experimental.pallas import tpu as pltpu
from jax.sharding import PartitionSpec as P

MESH = pl.DeviceIdType.MESH
LANES = 128
FIELD_ROWS = 8
MASS_ROW = 6
FLIPPED = (1, 0, 2)
COPIES = 2
UNROLL = 4
ROW = 8


def place(grid, lev, side):
    return {"grid": grid, "lev": lev, "side": side}


def exchange_kernel(
    sizes,
    cell_hbm,
    owner_hbm,
    block_owner_hbm,
    block_row_hbm,
    state_hbm,
    terrain_hbm,
    weight_hbm,
    landed_hbm,
    landed_owner_hbm,
    landed_row_hbm,
    rim_ref,
    owner_ref,
    state_ref,
    terrain_ref,
    weight_ref,
    rows,
    table,
    supply_rows,
    part,
    served,
    asked,
    parked,
    arrived,
    sums,
    sums_in,
    merged,
    merged_in,
    load_sem,
    park_send,
    park_recv,
    ask_send,
    ask_recv,
    owner_send,
    owner_recv,
    row_send,
    row_recv,
    value_send,
    value_recv,
    feed_send,
    feed_recv,
    sum_send,
    sum_recv,
    merged_send,
    merged_recv,
):
    tiles, groups, fields, cell_rows, slot_rows = sizes
    tile = lax.axis_index("grid")
    group = lax.axis_index("lev")
    side = lax.axis_index("side")
    partners = [
        lax.rem(tile + step, tiles) for step in (tiles - 1, 1, tiles // 2)
    ]
    peers = [lax.rem(group + step, groups) for step in range(1, groups)]
    row = min(ROW, tiles // 2)
    column = lax.rem(tile, row)
    before = lax.rem(tile + tiles - row, tiles)
    after = lax.rem(tile + row, tiles)
    late = lax.rem(tile + row - 1, tiles)
    keeper = lax.rem(tile + tiles - row + 1, tiles)
    steps = slot_rows // 2
    stride = 2 * cell_rows
    sent = pl.ds(0, fields + 1)
    span = fields * stride

    barrier = pltpu.get_barrier_semaphore()

    @pl.when(side == 0)
    def _():
        for partner, core in (
            (partners[0], 0), (partners[2], 0), (partners[0], 1), (partners[1], 1), (partners[2], 1)
        ):
            pl.semaphore_signal(
                barrier, inc=1, device_id=place(partner, group, core), device_id_type=MESH
            )

        @pl.when(column == row - 1)
        def _():
            pl.semaphore_signal(
                barrier, inc=1, device_id=place(keeper, group, 1), device_id_type=MESH
            )

    @pl.when(side == 1)
    def _():
        pl.semaphore_signal(
            barrier, inc=1, device_id=place(tile, group, 0), device_id_type=MESH
        )
        for peer in peers:
            pl.semaphore_signal(
                barrier, inc=1, device_id=place(tile, peer, 1), device_id_type=MESH
            )

        @pl.when(column == 0)
        def _():
            pl.semaphore_signal(
                barrier, inc=1, device_id=place(after, group, 0), device_id_type=MESH
            )

    load_state = pltpu.make_async_copy(state_hbm, state_ref, load_sem.at[0])
    load_terrain = pltpu.make_async_copy(terrain_hbm, terrain_ref, load_sem.at[1])
    load_weight = pltpu.make_async_copy(weight_hbm, weight_ref, load_sem.at[2])
    load_owner = pltpu.make_async_copy(owner_hbm, owner_ref, load_sem.at[3])
    load_state.start()
    load_terrain.start()

    def remote(source, target, sent, received, where):
        return pltpu.make_async_remote_copy(
            src_ref=source,
            dst_ref=target,
            send_sem=sent,
            recv_sem=received,
            device_id=where,
            device_id_type=MESH,
        )

    def ask(number, slot):
        return remote(
            cell_hbm, asked.at[slot], ask_send.at[number], ask_recv.at[slot],
            place(partners[number], group, 0),
        )

    def park(keeping):
        return remote(
            cell_hbm, parked.at[0], park_send.at[0], park_recv.at[0], place(keeping, group, 1)
        )

    def forward():
        return remote(
            parked.at[0], asked.at[FLIPPED[0]], ask_send.at[0], ask_recv.at[FLIPPED[0]],
            place(late, group, 0),
        )

    def tell_owner(number, slot):
        return remote(
            block_owner_hbm, landed_owner_hbm.at[slot], owner_send.at[number],
            owner_recv.at[slot], place(partners[number], group, 0),
        )

    def tell_row(number, slot):
        return remote(
            block_row_hbm, landed_row_hbm.at[slot], row_send.at[number],
            row_recv.at[slot], place(partners[number], group, 0),
        )

    row_number = lax.broadcasted_iota(jnp.int32, (FIELD_ROWS, LANES), 0)

    @pl.when(side == 0)
    def _():
        def serve(number, slot, step):
            return remote(
                served.at[number, step, :, sent], arrived.at[slot, step, :, sent],
                value_send.at[number, step], value_recv.at[slot, step], place(partners[number], group, 1 - side),
            )

        def feed(number, half):
            return remote(
                sums.at[half, :, sent], landed_hbm.at[number, half, :, sent], feed_send.at[number, half],
                feed_recv.at[number, half], place(partners[number], group, 1 - side),
            )

        @pl.when(column != 0)
        def _():
            pl.semaphore_wait(barrier, 3)

        @pl.when(column == 0)
        def _():
            pl.semaphore_wait(barrier, 4)
            park(before).start()

        for number in (1, 2):
            ask(number, FLIPPED[number]).start()
        for number in (1, 2):
            tell_owner(number, FLIPPED[number]).start()
            tell_row(number, FLIPPED[number]).start()
        load_terrain.wait()

        def fill(number, carry):
            mixed = jnp.zeros((FIELD_ROWS, LANES), jnp.float32)
            for member in range(4):
                lanes = pl.ds(pl.multiple_of((number * 4 + member) * LANES, LANES), LANES)
                turned = pltpu.roll(
                    terrain_ref[:, lanes].astype(jnp.float32),
                    lax.rem(2 * member + FIELD_ROWS - 2 * group, FIELD_ROWS),
                    axis=0,
                )
                mixed = jnp.where(row_number >> 1 == member, turned, mixed)
            supply_rows[pl.ds(pl.multiple_of(number * FIELD_ROWS, FIELD_ROWS), FIELD_ROWS), :] = (
                mixed
            )
            return carry

        lax.fori_loop(0, cell_rows // 4, fill, 0)
        load_state.wait()

        def split(number, carry):
            where = pl.ds(pl.multiple_of(number * stride, stride), stride)
            value = state_ref[where, :]
            high = value.astype(jnp.bfloat16)
            table[where, :LANES] = high
            table[where, LANES:] = (value - high.astype(jnp.float32)).astype(jnp.bfloat16)
            return carry

        lax.fori_loop(0, fields, split, 0)
        table[span:, :LANES] = supply_rows[...].astype(jnp.bfloat16)
        table[span:, LANES:] = jnp.zeros((stride, LANES), jnp.bfloat16)

        lane_number = lax.broadcasted_iota(jnp.int32, (LANES, LANES), 0)
        row_pair = lax.broadcasted_iota(jnp.int32, (stride, LANES), 0) >> 1
        for number in (1, 2, 0):
            ask(number, number).wait_recv()

            def look(step, carry):
                ones = []
                masks = []
                for half in range(2):
                    wanted = asked[number, 2 * step + half]
                    ones.append(
                        jnp.where(
                            lane_number
                            == jnp.broadcast_to(wanted & (LANES - 1), (LANES, LANES)),
                            1.0,
                            0.0,
                        ).astype(jnp.bfloat16)
                    )
                    masks.append(row_pair == jnp.broadcast_to(wanted >> 7, (stride, LANES)))
                one_hot = jnp.concatenate(ones, axis=1)
                one_hot = jnp.concatenate([one_hot, one_hot], axis=0)
                found = jnp.dot(table[...], one_hot, preferred_element_type=jnp.float32)
                for half in range(2):
                    tile_even = jnp.zeros((FIELD_ROWS, LANES), jnp.float32)
                    tile_odd = tile_even
                    for field in range(fields + 1):
                        picked = jnp.where(
                            masks[half],
                            found[
                                field * stride : (field + 1) * stride,
                                half * LANES : (half + 1) * LANES,
                            ],
                            0.0,
                        )
                        total = jnp.sum(
                            picked.reshape(stride // FIELD_ROWS, FIELD_ROWS, LANES), axis=0
                        )
                        total = total + pltpu.roll(total, 4, axis=0)
                        total = total + pltpu.roll(total, 2, axis=0)
                        other = pltpu.roll(total, 1, axis=0)
                        even, odd = (total, other) if field % 2 == 0 else (other, total)
                        tile_even = jnp.where(row_number == field, even, tile_even)
                        tile_odd = jnp.where(row_number == field, odd, tile_odd)
                    lanes = slice(half * LANES, (half + 1) * LANES)
                    served[number, step, 0, :, lanes] = tile_even
                    served[number, step, 1, :, lanes] = tile_odd
                serve(number, FLIPPED[number], step).start()
                return carry

            lax.fori_loop(0, steps, look, 0)
        @pl.when(column == 0)
        def _():
            park(before).wait_send()

        for number in (1, 2):
            ask(number, number).wait_send()
            tell_owner(number, number).wait_send()
            tell_row(number, number).wait_send()
        for number in range(3):
            tell_owner(number, number).wait_recv()
            tell_row(number, number).wait_recv()
            for step in range(steps):
                serve(number, number, step).wait_send()
        for half in range(2):
            for number in range(3):
                feed(number, half).wait_recv()

    @pl.when(side == 1)
    def _():
        load_weight.start()
        load_owner.start()
        rows[...] = jnp.broadcast_to(
            jnp.where(row_number == MASS_ROW, 1.0, 0.0)[None], rows.shape
        )
        load_state.wait()

        def fill(number, carry):
            for level in range(2):
                rows[level * cell_rows + number, 0:fields, :] = state_ref[
                    pl.ds(number * 2 + level, fields, stride=stride), :
                ]
            return carry

        lax.fori_loop(0, cell_rows, fill, 0, unroll=4)
        load_terrain.wait()
        load_weight.wait()
        levels = 2 * groups
        half_groups = cell_rows // 16
        lane_group = (
            lax.broadcasted_iota(jnp.int32, (levels * FIELD_ROWS, LANES), 1) >> 4
        )

        def block_group(half, step, carry):
            number = half * half_groups + step
            stack = []
            for member in range(8):
                block = number * 8 + member
                lanes = pl.ds(pl.multiple_of(block * LANES, LANES), LANES)
                low = rows[block]
                high = rows[cell_rows + block]
                supply = terrain_ref[:, lanes]
                for level in range(levels):
                    source = jnp.broadcast_to(supply[level : level + 1, :], (FIELD_ROWS, LANES))
                    stack.append(
                        jnp.where(
                            source == 2 * group,
                            low,
                            jnp.where(source == 2 * group + 1, high, 0.0),
                        )
                    )
            values = jnp.concatenate(stack, axis=0)
            coarse_part = values.astype(jnp.bfloat16)
            fine_part = (values - coarse_part.astype(jnp.float32)).astype(jnp.bfloat16)
            left = jnp.concatenate([coarse_part, fine_part], axis=1)
            weight = weight_ref[pl.ds(number * 8, 8)].reshape(8 * 16, LANES)
            weight_high = weight.astype(jnp.bfloat16)
            weight_low = (weight - weight_high.astype(jnp.float32)).astype(jnp.bfloat16)
            right = jnp.concatenate(
                [
                    jnp.concatenate([weight_high, weight_high], axis=1),
                    jnp.concatenate([weight_low, weight_low], axis=1),
                ],
                axis=0,
            )
            product = lax.dot_general(
                left, right, (((1,), (1,)), ((), ())), preferred_element_type=jnp.float32
            )
            total = jnp.zeros((levels * FIELD_ROWS, LANES), jnp.float32)
            for member in range(8):
                span = product[member * levels * FIELD_ROWS : (member + 1) * levels * FIELD_ROWS]
                total = jnp.where(
                    lane_group == member, span[:, :LANES] + span[:, LANES:], total
                )
            lanes = pl.ds(pl.multiple_of(step * LANES, LANES), LANES)
            for level in range(levels):
                part[half, level // 2, level % 2, :, lanes] = total[
                    level * FIELD_ROWS : (level + 1) * FIELD_ROWS
                ]
            return carry

        def sum_copy(number, half):
            return remote(
                part.at[half, peers[number], :, sent], sums_in.at[half, number, :, sent],
                sum_send.at[number, half], sum_recv.at[number, half],
                place(tile, peers[number], side),
            )

        def merged_copy(number, step):
            return remote(
                merged.at[step, :, pl.ds(0, fields)], merged_in.at[number, step, :, pl.ds(0, fields)],
                merged_send.at[number, step], merged_recv.at[number, step], place(tile, peers[number], side),
            )

        def feed(number, slot, half):
            return remote(
                sums.at[half, :, sent], landed_hbm.at[slot, half, :, sent], feed_send.at[number, half],
                feed_recv.at[slot, half], place(partners[number], group, 1 - side),
            )

        def serve(number, step):
            return remote(
                served.at[number, step, :, sent], arrived.at[number, step, :, sent],
                value_send.at[number, step], value_recv.at[number, step], place(partners[number], group, 1 - side),
            )

        lax.fori_loop(0, half_groups, functools.partial(block_group, 0), 0, unroll=UNROLL)
        @pl.when(column == 0)
        def _():
            pl.semaphore_wait(barrier, 4 + len(peers))
            park(before).wait_recv()
            forward().start()

        @pl.when(column != 0)
        def _():
            pl.semaphore_wait(barrier, 3 + len(peers))
            ask(0, FLIPPED[0]).start()

        for number in range(len(peers)):
            sum_copy(number, 0).start()
        tell_owner(0, FLIPPED[0]).start()
        tell_row(0, FLIPPED[0]).start()
        lax.fori_loop(0, half_groups, functools.partial(block_group, 1), 0, unroll=UNROLL)
        for number in range(len(peers)):
            sum_copy(number, 1).start()
        for half in range(2):
            for number in range(len(peers)):
                sum_copy(number, half).wait_recv()
            own = part[half, group]
            for number in range(len(peers)):
                own = own + sums_in[half, number]
            sums[half] = own
            for number in range(3):
                feed(number, FLIPPED[number], half).start()
        load_owner.wait()
        for step in range(steps):
            for number in range(3):
                serve(number, step).wait_recv()
            for half in range(2):
                lanes = slice(half * LANES, (half + 1) * LANES)
                owner = jnp.broadcast_to(owner_ref[2 * step + half], (FIELD_ROWS, LANES))
                for level in range(2):
                    merged[step, level, :, lanes] = jnp.where(
                        owner == partners[0],
                        arrived[0, step, level, :, lanes],
                        jnp.where(
                            owner == partners[1],
                            arrived[1, step, level, :, lanes],
                            arrived[2, step, level, :, lanes],
                        ),
                    )
            for number in range(len(peers)):
                merged_copy(number, step).start()
        for step in range(steps):
            for number in range(len(peers)):
                merged_copy(number, step).wait_recv()
            for half in range(2):
                lanes = slice(half * LANES, (half + 1) * LANES)
                slot_lanes = slice((2 * step + half) * LANES, (2 * step + half + 1) * LANES)
                for level in range(2):
                    wanted = jnp.broadcast_to(
                        merged[step, level, fields : fields + 1, lanes], (FIELD_ROWS, LANES)
                    )
                    value = jnp.zeros((FIELD_ROWS, LANES), jnp.float32)
                    for there in range(2):
                        value = jnp.where(
                            wanted == (2 * group + there).astype(jnp.float32),
                            merged[step, there, :, lanes],
                            value,
                        )
                        for number in range(len(peers)):
                            origin = lax.rem(group + groups - 1 - number, groups)
                            value = jnp.where(
                                wanted == (2 * origin + there).astype(jnp.float32),
                                merged_in[number, step, there, :, lanes],
                                value,
                            )
                    rim_ref[level, :, slot_lanes] = value
        @pl.when(column == 0)
        def _():
            forward().wait_send()

        @pl.when(column != 0)
        def _():
            ask(0, FLIPPED[0]).wait_send()

        tell_owner(0, FLIPPED[0]).wait_send()
        tell_row(0, FLIPPED[0]).wait_send()
        for number in range(len(peers)):
            for half in range(2):
                sum_copy(number, half).wait_send()
            for step in range(steps):
                merged_copy(number, step).wait_send()
        for number in range(3):
            for half in range(2):
                feed(number, FLIPPED[number], half).wait_send()


def finish_kernel(
    sizes, owner_any, run_any, state_ref, landed_ref, rim_ref, out_hbm, result, owner_ref, run_ref,
    sems, list_sem, *totals
):
    fields, cell_rows, slot_rows, blocks = sizes
    tile = lax.axis_index("grid")
    side = lax.axis_index("side")
    stride = 2 * cell_rows
    rim_rows = 2 * slot_rows
    half_groups = cell_rows // 16

    def put(source, field, first, count, slot):
        where = pl.ds(field * stride + first, count)
        return pltpu.make_async_copy(source.at[where], out_hbm.at[where], sems.at[slot, field])

    @pl.when(side == 0)
    def _():
        lists = [
            pltpu.make_async_copy(owner_any, owner_ref, list_sem.at[0]),
            pltpu.make_async_copy(run_any, run_ref, list_sem.at[1]),
        ]
        for copy in lists:
            copy.start()
        for total in totals:
            total[...] = jnp.zeros_like(total)
        for copy in lists:
            copy.wait()
        lane_group = lax.broadcasted_iota(jnp.int32, (FIELD_ROWS, LANES), 1) >> 4
        for number in range(3):
            for half in range(2):

                def add(step, carry):
                    lanes = pl.ds(pl.multiple_of(step * LANES, LANES), LANES)
                    sources = [landed_ref[number, half, level, :, lanes] for level in range(2)]
                    places = []
                    moved = []
                    for member in range(8):
                        block = (half * half_groups + step) * 8 + member
                        run = run_ref[number, 0, block]
                        target = run & 7
                        shift = ((target - member) & 7) * 16
                        inside = lane_group == target
                        moved.append(
                            [
                                jnp.where(inside, pltpu.roll(source, shift, axis=1), 0.0)
                                for source in sources
                            ]
                        )
                        row = jnp.where(owner_ref[number, 0, block] == tile, run >> 3, cell_rows)
                        places.append(pl.ds(pl.multiple_of(row * FIELD_ROWS, FIELD_ROWS), FIELD_ROWS))
                    for member in range(8):
                        for level in range(2):
                            total = totals[(member % COPIES) * 2 + level]
                            where = places[member]
                            total[where, :] = total[where, :] + moved[member][level]
                    return carry

                lax.fori_loop(0, half_groups, add, 0, unroll=UNROLL)

        def gathered(level, row):
            value = totals[level][pl.ds(row, cell_rows, stride=FIELD_ROWS), :]
            for copy in range(1, COPIES):
                value = value + totals[copy * 2 + level][
                    pl.ds(row, cell_rows, stride=FIELD_ROWS), :
                ]
            return value

        scale = 1.0 / (1.0 + gathered(0, MASS_ROW))
        for field in range(fields):
            for level in range(2):
                where = pl.ds(field * stride + level, cell_rows, stride=2)
                result[where, :] = (state_ref[where, :] + gathered(level, field)) * scale
            put(result, field, 0, stride, 0).start()
        for field in range(fields):
            put(result, field, 0, stride, 0).wait()

    @pl.when(side == 1)
    def _():
        for field in range(fields):
            put(state_ref, field, rim_rows, stride - rim_rows, 0).start()
        for number in range(slot_rows):
            for level in range(2):
                where = pl.ds(number * 2 + level, fields, stride=stride)
                result[where, :] = 0.5 * (
                    state_ref[where, :]
                    + rim_ref[level, 0:fields, number * LANES : (number + 1) * LANES]
                )
        for field in range(fields):
            put(result, field, 0, rim_rows, 1).start()
        for field in range(fields):
            put(state_ref, field, rim_rows, stride - rim_rows, 0).wait()
            put(result, field, 0, rim_rows, 1).wait()


def on_device(
    tiles, groups,
    model_state, terrain_level, panel_owner, panel_cell, block_weight, block_owner, block_row
):
    _, lev_dev, fields, cells = model_state.shape
    cell_rows = cells // LANES
    slots = panel_cell.shape[0]
    slot_rows = slots // LANES
    blocks = block_row.shape[0]
    state = (
        model_state[0]
        .transpose(1, 0, 2)
        .reshape(fields, lev_dev, cell_rows, LANES)
        .transpose(0, 2, 1, 3)
        .reshape(fields * cell_rows * lev_dev, LANES)
    )
    cell_wanted = panel_cell.reshape(slot_rows, 1, LANES)
    cell_owner = panel_owner.reshape(slot_rows, 1, LANES)
    run_owner = block_owner.reshape(1, blocks)
    run_row = block_row.reshape(1, blocks)
    vmem = pl.BlockSpec(memory_space=pltpu.VMEM)
    free = pl.BlockSpec(memory_space=pl.ANY)
    hbm = pl.BlockSpec(memory_space=pl.ANY)
    tile_shape = (2, FIELD_ROWS, slots)
    steps = slot_rows // 2
    chunks = (steps, 2, FIELD_ROWS, 2 * LANES)
    halves = (2, 2, FIELD_ROWS, blocks * 8)
    dma = pltpu.SemaphoreType.DMA
    landed, landed_owner, landed_row, rim = pl.pallas_call(
        functools.partial(
            exchange_kernel, (tiles, groups, fields, cell_rows, slot_rows)
        ),
        out_shape=(
            jax.ShapeDtypeStruct((3, *halves), jnp.float32),
            jax.ShapeDtypeStruct((3, 1, blocks), jnp.int32),
            jax.ShapeDtypeStruct((3, 1, blocks), jnp.int32),
            jax.ShapeDtypeStruct(tile_shape, jnp.float32),
        ),
        in_specs=[hbm] * 7,
        out_specs=(hbm, hbm, hbm, vmem),
        scratch_shapes=[
            pltpu.VMEM((slot_rows, 1, LANES), jnp.int32),
            pltpu.VMEM(state.shape, jnp.float32),
            pltpu.VMEM(terrain_level.shape[1:], jnp.int32),
            pltpu.VMEM(block_weight.shape, jnp.float32),
            pltpu.VMEM((2 * cell_rows, FIELD_ROWS, LANES), jnp.float32),
            pltpu.VMEM(((fields + 1) * 2 * cell_rows, 2 * LANES), jnp.bfloat16),
            pltpu.VMEM((2 * cell_rows, LANES), jnp.float32),
            pltpu.VMEM((2, groups, *halves[1:]), jnp.float32),
            pltpu.VMEM((3, *chunks), jnp.float32),
            pltpu.VMEM((3, slot_rows, 1, LANES), jnp.int32),
            pltpu.VMEM((1, slot_rows, 1, LANES), jnp.int32),
            pltpu.VMEM((3, *chunks), jnp.float32),
            pltpu.VMEM(halves, jnp.float32),
            pltpu.VMEM((2, groups - 1, *halves[1:]), jnp.float32),
            pltpu.VMEM(chunks, jnp.float32),
            pltpu.VMEM((groups - 1, *chunks), jnp.float32),
            dma((4,)),
            dma((1,)),
            dma((1,)),
            *[dma((3,))] * 6,
            *[dma((3, steps))] * 2,
            *[dma((3, 2))] * 2,
            *[dma((groups - 1, 2))] * 2,
            *[dma((groups - 1, steps))] * 2,
        ],
        compiler_params=pltpu.CompilerParams(collective_id=0, has_side_effects=True, vmem_limit_bytes=16 * 1024 * 1024),
    )(*(pltpu.with_memory_space_constraint(x, pltpu.HBM) for x in (cell_wanted, cell_owner, run_owner, run_row, state, terrain_level[0], block_weight)))
    out = pl.pallas_call(
        functools.partial(finish_kernel, (fields, cell_rows, slot_rows, blocks)),
        out_shape=jax.ShapeDtypeStruct(state.shape, jnp.float32),
        in_specs=[free, free, vmem, vmem, vmem],
        out_specs=pl.BlockSpec(memory_space=pl.ANY),
        compiler_params=pltpu.CompilerParams(vmem_limit_bytes=8 * 1024 * 1024),
        scratch_shapes=[
            pltpu.VMEM(state.shape, jnp.float32),
            pltpu.SMEM((3, 1, blocks), jnp.int32),
            pltpu.SMEM((3, 1, blocks), jnp.int32),
            dma((2, fields)),
            dma((2,)),
            *[pltpu.VMEM(((cell_rows + 1) * FIELD_ROWS, LANES), jnp.float32)] * (2 * COPIES),
        ],
    )(landed_owner, landed_row, state, landed, rim)
    out = (
        out.reshape(fields, cell_rows, lev_dev, LANES)
        .transpose(0, 2, 1, 3)
        .reshape(fields, lev_dev, cells)
        .transpose(1, 0, 2)
    )
    return out[None]


def solution(mesh):
    in_specs = (
        P("side", "lev", None, "grid"),
        P("side", None, "grid"),
        P("grid", None),
        P("grid"),
        P("grid", None, None),
        P("grid", None),
        P("grid"),
    )
    out_specs = P("side", "lev", None, "grid")
    return jax.shard_map(
        functools.partial(on_device, mesh.shape["grid"], mesh.shape["lev"]),
        mesh=mesh,
        in_specs=in_specs,
        out_specs=out_specs,
        check_vma=False,
    )
```
